128 devices in a mesh: depth: 16 (over z_hi, y, core), lat: 8 (over x, z_lo).
Axes of the slice: x: 4, y: 4, z: 4 (z_hi: 2, z_lo: 2; z = z_hi * 2 + z_lo), core: 2. Of those that a mesh axis runs over, the one named last changes fastest.
Arguments:
- rhs_field: float32 [2, 32, 8, 8192], P(None, 'depth', None, 'lat'), may hold values from -4 to 4
- src_cell: int32 [8], replicated, may hold values from 0 to 8191
- src_layer: int32 [8], replicated, may hold values from 0 to 31
- factor: float32 [32, 64, 3, 2, 128, 128], P('depth', 'lat'), as said below
- couple: float32 [2, 2, 32, 8192], P(None, None, 'depth', 'lat')
Outputs:
- waves: float32 [2, 32, 8, 8192], P(None, 'depth', None, 'lat')
- field: float32 [2, 32, 8, 8192], P(None, 'depth', None, 'lat')
The draws below stay inside these ranges and needn't reach their ends.
Inputs may be any that keep to these rules, and one draw needn't show every extreme that they name: The centre block of every factor is a complex diagonal of modulus 0.92 plus independent entries; the others are independent entries.
All inputs are finite; a program needn't handle non-finite values.
Results may differ from the reference program's by a relative error of at most 0.0003.
Values sent between devices are 32-bit elements; how exact they have to be, the bound alone decides.
No kernel may reach another device: no remote copies, remote signals or barrier semaphores. Data moves between devices by JAX's collectives and lax.ppermute only.
A program may use at most 128 MiB of HBM per device.

```python
import math
import jax
import jax.numpy as jnp
from jax import lax

TILE = 128
SHOTS = 8
LAYERS = 32
TILES = 64
LATERAL = 8192


def draw_factor(key, part):
    key_one = jax.random.fold_in(key, 11)
    key_two = jax.random.fold_in(key, 12)
    shape = (LAYERS, TILES, 3, 2, TILE, TILE)
    sigma = math.sqrt(0.16 / (6.0 * TILE))
    random_part = jax.random.normal(key_one, shape, jnp.float32) * sigma
    phase_angle = jax.random.uniform(key_two, (LAYERS, TILES, 1, 1, TILE, 1), jnp.float32, -math.pi, math.pi)
    row_ids = jnp.arange(TILE, dtype=jnp.int32)
    unit_diag = (row_ids[:, None] == row_ids[None, :]).astype(jnp.float32).reshape(1, 1, 1, 1, TILE, TILE)
    centre_flag = (jnp.arange(3, dtype=jnp.int32) == 1).astype(jnp.float32).reshape(1, 1, 3, 1, 1, 1)
    part_flag = jnp.arange(2, dtype=jnp.int32).reshape(1, 1, 1, 2, 1, 1)
    rotation = jnp.where(part_flag == 0, jnp.cos(phase_angle), jnp.sin(phase_angle))
    return random_part + 0.92 * unit_diag * centre_flag * rotation


def draw_couple(key, part):
    key_one = jax.random.fold_in(key, 21)
    key_two = jax.random.fold_in(key, 22)
    shape = (2, 1, LAYERS, LATERAL)
    modulus = jax.random.uniform(key_one, shape, jnp.float32, 0.9, 1.0)
    phase_angle = jax.random.uniform(key_two, shape, jnp.float32, -math.pi, math.pi)
    return jnp.concatenate([modulus * jnp.cos(phase_angle), modulus * jnp.sin(phase_angle)], axis=1)


def with_ends(entries, own_key, least, largest):
    spot = [jax.random.randint(jax.random.fold_in(own_key, axis), (), 0, length) for axis, length in enumerate(entries.shape)]
    widest = entries.shape.index(max(entries.shape))
    neighbour = spot[:widest] + [(spot[widest] + 1) % entries.shape[widest]] + spot[widest + 1:]
    return entries.at[tuple(spot)].set(least).at[tuple(neighbour)].set(largest)


def level_of(key, shape, shards, low, high):
    gain, own = 1.0, jax.random.fold_in(key, 6)
    for dim, blocks in shards:
        draws = jnp.exp(jax.random.uniform(jax.random.fold_in(own, dim), (blocks,), jnp.float32, low / len(shards), high / len(shards)))
        gain = gain * jnp.repeat(draws, shape[dim] // blocks).reshape([-1 if axis == dim else 1 for axis in range(len(shape))])
    return gain


def noise(key, dims, scale, most, cuts=(), held_as=jnp.bfloat16):
    array = jax.random.normal(key, dims, jnp.float32) * scale
    if len(cuts) > 0:
        array = level_of(key, dims, cuts, -0.22, 0.18) * array
    return jnp.clip(array, min=-most, max=most).astype(held_as)


def setup_inputs(seed: int = 0) -> dict:
    key_list = jax.random.split(jax.random.key(seed), 6)
    rhs_field = noise(key_list[0], (2, LAYERS, SHOTS, LATERAL), 0.5, 4.0, ((1, 16), (3, 8)), jnp.float32)
    src_cell = with_ends(jax.random.randint(key_list[1], (SHOTS,), 0, LATERAL), jax.random.fold_in(key_list[1], 1), 0, LATERAL - 1).astype(jnp.int32)
    src_layer = with_ends(jax.random.randint(key_list[2], (SHOTS,), 0, LAYERS), jax.random.fold_in(key_list[2], 1), 0, LAYERS - 1).astype(jnp.int32)
    factor = draw_factor(jax.random.fold_in(key_list[5], 71), 0)
    couple = draw_couple(jax.random.fold_in(key_list[5], 71), 0)
    return dict(rhs_field=rhs_field, src_cell=src_cell, src_layer=src_layer, factor=factor, couple=couple)


def complex_scale(coef, vector):
    real_part = coef[0][None, :] * vector[0] - coef[1][None, :] * vector[1]
    imag_part = coef[0][None, :] * vector[1] + coef[1][None, :] * vector[0]
    return jnp.stack([real_part, imag_part])


def apply_blocks(vector, blocks):
    tile_cells = blocks.shape[-1]
    line_cells = vector.shape[-1]
    tile_count = line_cells // tile_cells
    shot_count = vector.shape[1]
    padded = jnp.pad(vector, ((0, 0), (0, 0), (tile_cells, tile_cells)))
    shifted = jnp.stack([padded[:, :, offset * tile_cells: offset * tile_cells + line_cells].reshape(2, shot_count, tile_count, tile_cells) for offset in range(3)], axis=3)
    form = "stjp,tjpq->stq"
    high = lax.Precision.HIGHEST
    real_out = jnp.einsum(form, shifted[0], blocks[:, :, 0], precision=high) - jnp.einsum(form, shifted[1], blocks[:, :, 1], precision=high)
    imag_out = jnp.einsum(form, shifted[0], blocks[:, :, 1], precision=high) + jnp.einsum(form, shifted[1], blocks[:, :, 0], precision=high)
    return jnp.stack([real_out, imag_out]).reshape(2, shot_count, line_cells)


def reference(rhs_field, src_cell, src_layer, factor, couple):
    layer_ids = jnp.arange(LAYERS, dtype=jnp.int32)
    cell_ids = jnp.arange(LATERAL, dtype=jnp.int32)
    hit = (src_layer[None, :, None] == layer_ids[:, None, None]) & (src_cell[None, :, None] == cell_ids[None, None, :])
    real_part = rhs_field[0] + 4.0 * hit.astype(jnp.float32)
    forcing = jnp.stack([real_part, rhs_field[1]])
    layer_forcing = jnp.moveaxis(forcing, 1, 0)
    couple_down = jnp.moveaxis(couple[0], 1, 0)
    couple_up = jnp.moveaxis(couple[1], 1, 0)

    def down_step(carried, inputs):
        source, blocks, coef = inputs
        new_wave = apply_blocks(source + complex_scale(coef, carried), blocks)
        return new_wave, new_wave

    start_wave = jnp.zeros((2, SHOTS, LATERAL), jnp.float32)
    _, wave_layers = lax.scan(down_step, start_wave, (layer_forcing, factor, couple_down))

    def up_step(carried, inputs):
        wave, blocks, coef = inputs
        new_field = wave + apply_blocks(complex_scale(coef, carried), blocks)
        return new_field, new_field

    _, field_layers = lax.scan(up_step, start_wave, (wave_layers, factor, couple_up), reverse=True)
    return jnp.moveaxis(wave_layers, 0, 1), jnp.moveaxis(field_layers, 0, 1)
```

```python
import functools

import jax
import jax.numpy as jnp
from jax import lax
from jax.experimental import pallas as pl
from jax.experimental.pallas import tpu as pltpu
from jax.sharding import PartitionSpec as P

TILE = 128
GROUP = 4
OWN = 4
HALO = 3
SLOTS = OWN + 2 * HALO
WINDOW = (OWN + 2 * (HALO + 1)) * TILE
SPAN = SLOTS * TILE
HALF = OWN * TILE
VMEM_LIMIT = 10 << 20

VMEM_SPEC = pl.BlockSpec(memory_space=pltpu.VMEM)
SMEM_SPEC = pl.BlockSpec(memory_space=pltpu.SMEM)
ANY_SPEC = pl.BlockSpec(memory_space=pl.ANY)
PARAMS = pltpu.CompilerParams(vmem_limit_bytes=VMEM_LIMIT)
AXES = ("depth", "lat")


def split_store(buffer, slot_ref):
    for offset in range(3):
        for part in range(2):
            block = buffer[offset, part]
            high = block.astype(jnp.bfloat16)
            low = (block - high.astype(jnp.float32)).astype(jnp.bfloat16)
            rows = slice(offset * TILE, (offset + 1) * TILE)
            slot_ref[rows, part * TILE : (part + 1) * TILE] = high
            slot_ref[rows, (2 + part) * TILE : (3 + part) * TILE] = low


def pipelined(units, source_of, slot_of, buffers, sems):
    def copy(unit, place):
        return pltpu.make_async_copy(source_of(unit), buffers.at[place], sems.at[place])

    copy(0, 0).start()

    def body(unit, _):
        place = lax.rem(unit, 2)

        @pl.when(unit + 1 < units)
        def _():
            copy(unit + 1, 1 - place).start()

        copy(unit, place).wait()
        split_store(buffers.at[place], slot_of(unit))
        return 0

    lax.fori_loop(0, units, body, 0)


def chip_body(ids, source, *refs, mine):
    packed, buffers, sems = refs[-3:]
    core = ids[1]
    first = 2 * core if mine else 2 * (1 - core)
    count = OWN + HALO

    def source_of(unit):
        return source.at[unit // count, lax.rem(unit, count) + core]

    def slot_of(unit):
        return packed.at[first + unit // count, lax.rem(unit, count) + HALO * (1 - core)]

    pipelined(2 * count, source_of, slot_of, buffers, sems)


def halo_body(ids, *refs, places):
    sources = refs[:4]
    packed, buffers, sems = refs[-3:]
    core = ids[1]
    for side in range(2):

        @pl.when(core == side)
        def _():
            units = []
            for near, entries in ((sources[side], places[0]), (sources[2 + side], places[1])):
                for index, (layer, reach) in enumerate(entries[side]):
                    units.append((near.at[index], packed.at[layer, reach]))

            def copy(number):
                place = number % 2
                return pltpu.make_async_copy(units[number][0], buffers.at[place], sems.at[place])

            copy(0).start()
            for number in range(len(units)):
                if number + 1 < len(units):
                    copy(number + 1).start()
                copy(number).wait()
                split_store(buffers.at[number % 2], units[number][1])


PACKED = (GROUP, SLOTS, 3 * TILE, 4 * TILE)
PACK_SCRATCH = [pltpu.VMEM((2, 3, 2, TILE, TILE), jnp.float32), pltpu.SemaphoreType.DMA((2,))]


def pack_chip(ids, source, packed, mine):
    extra = () if packed is None else (packed,)
    return pl.pallas_call(
        functools.partial(chip_body, mine=mine),
        in_specs=[SMEM_SPEC, ANY_SPEC] + [VMEM_SPEC] * len(extra),
        out_specs=VMEM_SPEC,
        out_shape=jax.ShapeDtypeStruct(PACKED, jnp.bfloat16),
        scratch_shapes=PACK_SCRATCH,
        input_output_aliases={2: 0} if extra else {},
        compiler_params=PARAMS,
        name="pack_mine" if mine else "pack_partner",
    )(ids, source, *extra)


def pack_halo(ids, sources, packed, places, name):
    return pl.pallas_call(
        functools.partial(halo_body, places=places),
        in_specs=[SMEM_SPEC] + [ANY_SPEC] * 4 + [VMEM_SPEC],
        out_specs=VMEM_SPEC,
        out_shape=jax.ShapeDtypeStruct(PACKED, jnp.bfloat16),
        scratch_shapes=PACK_SCRATCH,
        input_output_aliases={5: 0},
        compiler_params=PARAMS,
        name=name,
    )(ids, *sources, packed)


def store_parts(parts_ref, where, value):
    high = value.astype(jnp.bfloat16)
    parts_ref[0:16, where] = high
    parts_ref[16:32, where] = (value - high.astype(jnp.float32)).astype(jnp.bfloat16)


def scaled(coef_real, coef_imag, value):
    real, imag = value[0:8], value[8:16]
    return jnp.concatenate(
        [coef_real * real - coef_imag * imag, coef_real * imag + coef_imag * real], axis=0
    )


def tile_product(parts_ref, packed, layer, spot):
    product = jnp.dot(
        parts_ref[:, spot * TILE : (spot + 3) * TILE],
        packed[layer, spot],
        preferred_element_type=jnp.float32,
    )
    rows = product[0:16] + product[16:32]
    both = rows[:, 0 : 2 * TILE] + rows[:, 2 * TILE : 4 * TILE]
    real, imag = both[0:8], both[8:16]
    return jnp.concatenate(
        [real[:, 0:TILE] - imag[:, TILE:], real[:, TILE:] + imag[:, 0:TILE]], axis=0
    )


def lanes(start, stop):
    return slice(start * TILE, stop * TILE)


def down_body(ids, low, mid, high, window, packed, _, out, waves, parts, *, turn):
    @pl.when(ids[0] == turn)
    def _():
        for layer in range(GROUP):
            reach = HALO - layer
            if layer == 0:
                pieces = [(lanes(0, 4), low[...]), (lanes(4, 8), mid[...]), (lanes(8, 12), high[...])]
            else:
                begin, end = HALO - reach - 1, HALO + OWN + reach + 1
                pieces = [(lanes(begin + 1, end + 1), waves[layer - 1, :, lanes(begin, end)])]
            for where, value in pieces:
                forcing = window[layer, 0:16, where]
                coef_real = window[layer, 16:17, where]
                coef_imag = window[layer, 17:18, where]
                store_parts(parts, where, forcing + scaled(coef_real, coef_imag, value))
            for spot in range(HALO - reach, HALO + OWN + reach):
                waves[layer, :, lanes(spot, spot + 1)] = tile_product(parts, packed, layer, spot)
        out[...] = waves[GROUP - 1, :, lanes(HALO, HALO + OWN)]


def up_body(ids, low, mid, high, window, packed, waves, left, right, _, out, field, parts, span, *, turn):
    @pl.when(ids[0] == turn)
    def _():
        for layer in reversed(range(GROUP)):
            reach = layer
            if layer == GROUP - 1:
                pieces = [(lanes(0, 4), low[...]), (lanes(4, 8), mid[...]), (lanes(8, 12), high[...])]
            else:
                begin, end = HALO - reach - 1, HALO + OWN + reach + 1
                pieces = [(lanes(begin + 1, end + 1), span[:, lanes(begin, end)])]
            for where, value in pieces:
                coef_real = window[layer, 18:19, where]
                coef_imag = window[layer, 19:20, where]
                store_parts(parts, where, scaled(coef_real, coef_imag, value))
            for spot in range(HALO - reach, HALO + OWN + reach):
                if layer >= 2 and spot < HALO:
                    wave = left[layer - 2, :, lanes(spot + 1, spot + 2)]
                elif layer >= 2 and spot >= HALO + OWN:
                    wave = right[layer - 2, :, lanes(spot - HALO - OWN, spot - HALO - OWN + 1)]
                else:
                    wave = waves[layer, :, lanes(spot, spot + 1)]
                span[:, lanes(spot, spot + 1)] = wave + tile_product(parts, packed, layer, spot)
            field[layer] = span[:, lanes(HALO, HALO + OWN)]
        out[...] = span[:, lanes(HALO, HALO + OWN)]


PARTS = pltpu.VMEM((32, WINDOW), jnp.bfloat16)


def down_step(ids, received, window, packed, waves, turn):
    return pl.pallas_call(
        functools.partial(down_body, turn=turn),
        in_specs=[SMEM_SPEC] + [VMEM_SPEC] * 6,
        out_specs=(VMEM_SPEC, VMEM_SPEC),
        out_shape=(
            jax.ShapeDtypeStruct((16, HALF), jnp.float32),
            jax.ShapeDtypeStruct((GROUP, 16, SPAN), jnp.float32),
        ),
        scratch_shapes=[PARTS],
        input_output_aliases={6: 1},
        compiler_params=PARAMS,
        name=f"down_{turn}",
    )(ids, *received, window, packed, waves)


def up_step(ids, received, window, packed, waves, left, right, field, turn):
    return pl.pallas_call(
        functools.partial(up_body, turn=turn),
        in_specs=[SMEM_SPEC] + [VMEM_SPEC] * 9,
        out_specs=(VMEM_SPEC, VMEM_SPEC),
        out_shape=(
            jax.ShapeDtypeStruct((16, HALF), jnp.float32),
            jax.ShapeDtypeStruct((GROUP, 16, HALF), jnp.float32),
        ),
        scratch_shapes=[PARTS, pltpu.VMEM((16, SPAN), jnp.float32)],
        input_output_aliases={9: 1},
        compiler_params=PARAMS,
        name=f"up_{turn}",
    )(ids, *received, window, packed, waves, left, right, field)


def shards(rhs_field, src_cell, src_layer, factor, couple):
    layer_total, shot_count, strip_cells = rhs_field.shape[1:]
    depth_count, lat_count = lax.axis_size("depth"), lax.axis_size("lat")
    depth_pos, lat_pos = lax.axis_index("depth"), lax.axis_index("lat")
    core = lax.rem(depth_pos, 2)
    first_core = core == 0
    chip_rows = depth_count // 2
    halves = 2 * lat_count
    ids = jnp.stack([depth_pos // 2, core]).astype(jnp.int32)

    def device(row, half):
        return (2 * row + half % 2) * lat_count + half // 2

    def at(depth, lat):
        return depth * lat_count + lat

    def hop(value, rows, step, shift):
        pairs = [
            (device(row, half), device(row + step, half + shift))
            for row in rows
            if 0 <= row + step < chip_rows
            for half in range(halves)
            if 0 <= half + shift < halves
        ]
        return lax.ppermute(value, AXES, pairs)

    partner = [(at(d, l), at(d ^ 1, l)) for d in range(depth_count) for l in range(lat_count)]

    def outward(value, sender, right):
        target, shift = (0, 1) if right else (1, -1)
        pairs = [
            (at(2 * row + sender, l), at(2 * row + target, l + shift))
            for row in range(chip_rows)
            for l in range(lat_count)
            if 0 <= l + shift < lat_count
        ]
        return lax.ppermute(value, AXES, pairs)

    other = lax.ppermute(factor, AXES, partner)
    tiles = factor.shape[1]
    two_right = jnp.concatenate([factor[0, tiles - 3 :], factor[1, tiles - 2 :]])
    two_left = jnp.concatenate([factor[0, :3], factor[1, :2]])
    near_down = (
        outward(two_right, 0, True),
        outward(two_left, 0, False),
        outward(factor[0, tiles - 1 :], 1, True),
        outward(factor[0, :1], 1, False),
    )
    four_right = jnp.concatenate([factor[1, tiles - 3 :], factor[0, tiles - 2 : tiles - 1]])
    four_left = jnp.concatenate([factor[1, :3], factor[0, 1:2]])

    layer_ids = depth_pos * layer_total + jnp.arange(layer_total, dtype=jnp.int32)
    cell_ids = lat_pos * strip_cells + jnp.arange(strip_cells, dtype=jnp.int32)
    hit = (src_layer[None, :, None] == layer_ids[:, None, None]) & (
        src_cell[None, :, None] == cell_ids[None, None, :]
    )
    real_part = rhs_field[0] + 4.0 * hit.astype(jnp.float32)
    rows = jnp.concatenate(
        [real_part, rhs_field[1]] + [couple[way, part][:, None] for way in range(2) for part in range(2)],
        axis=1,
    )
    rows_other = lax.ppermute(rows, AXES, partner)
    chip = jnp.concatenate(
        [jnp.where(first_core, rows, rows_other), jnp.where(first_core, rows_other, rows)]
    )
    edge = jnp.where(first_core, chip[..., HALF:], chip[..., :HALF])
    straight = [(at(2 * r, l), at(2 * r, l + 1)) for r in range(chip_rows) for l in range(lat_count - 1)] + [
        (at(2 * r + 1, l), at(2 * r + 1, l - 1)) for r in range(chip_rows) for l in range(1, lat_count)
    ]
    beside = lax.ppermute(edge, AXES, straight)
    window = jnp.where(
        first_core,
        jnp.concatenate([beside, chip], axis=-1),
        jnp.concatenate([chip, beside], axis=-1),
    )

    packed = pack_chip(ids, factor, None, True)
    packed = pack_chip(ids, other, packed, False)
    down_places = (
        (((0, 0), (0, 1), (0, 2), (1, 1), (1, 2)), ((0, 7), (0, 8), (0, 9), (1, 7), (1, 8))),
        (((2, 2),), ((2, 7),)),
    )
    packed = pack_halo(ids, near_down, packed, down_places, "halo_down")

    zero_half = jnp.zeros((2 * shot_count, HALF), jnp.float32)
    waves = jnp.zeros((GROUP, 2 * shot_count, SPAN), jnp.float32)
    field = jnp.zeros((GROUP, 2 * shot_count, HALF), jnp.float32)

    received = (zero_half,) * 3
    for turn in range(chip_rows):
        out, waves = down_step(ids, received, window, packed, waves, turn)
        if turn + 1 < chip_rows:
            group = range(turn % 3, chip_rows, 3)
            received = (hop(out, group, 1, 1), hop(out, group, 1, 0), hop(out, group, 1, -1))

    near_up = (outward(four_right, 1, True), outward(four_left, 1, False))
    up_places = (
        (((3, 0), (3, 1), (3, 2), (2, 1)), ((3, 7), (3, 8), (3, 9), (2, 8))),
        ((), ()),
    )
    packed = pack_halo(ids, near_up + near_up, packed, up_places, "halo_up")

    deep = waves[2:, :, HALO * TILE : (HALO + OWN) * TILE]
    everyone = range(chip_rows)
    left, right = hop(deep, everyone, 0, 1), hop(deep, everyone, 0, -1)
    received = (zero_half,) * 3
    for turn in reversed(range(chip_rows)):
        out, field = up_step(ids, received, window, packed, waves, left, right, field, turn)
        if turn:
            group = range(turn % 3, chip_rows, 3)
            received = (hop(out, group, -1, 1), hop(out, group, -1, 0), hop(out, group, -1, -1))

    own_waves = waves[:, :, HALO * TILE : (HALO + OWN) * TILE]
    both = jnp.stack([own_waves, field])
    keep = jnp.where(first_core, both[:, :2], both[:, 2:])
    give = jnp.where(first_core, both[:, 2:], both[:, :2])
    taken = lax.ppermute(give, AXES, partner)
    whole = jnp.concatenate(
        [jnp.where(first_core, keep, taken), jnp.where(first_core, taken, keep)], axis=-1
    )
    whole = whole.reshape(2, layer_total, 2, shot_count, strip_cells).transpose(0, 2, 1, 3, 4)
    return (whole[0], whole[1])


def solution(mesh):
    placed = (
        P(None, "depth", None, "lat"),
        P(),
        P(),
        P("depth", "lat", None, None, None, None),
        P(None, None, "depth", "lat"),
    )
    return jax.shard_map(
        shards,
        mesh=mesh,
        in_specs=placed,
        out_specs=(P(None, "depth", None, "lat"), P(None, "depth", None, "lat")),
        check_vma=False,
    )
```

```python
import functools

import jax
import jax.numpy as jnp
from jax import lax
from jax.experimental import pallas as pl
from jax.experimental.pallas import tpu as pltpu
from jax.sharding import PartitionSpec as P

TILE = 128
GROUP = 4
OWN = 4
HALO = 3
SLOTS = OWN + 2 * HALO
WINDOW = (OWN + 2 * (HALO + 1)) * TILE
SPAN = SLOTS * TILE
HALF = OWN * TILE
VMEM_LIMIT = 10 << 20

VMEM_SPEC = pl.BlockSpec(memory_space=pltpu.VMEM)
SMEM_SPEC = pl.BlockSpec(memory_space=pltpu.SMEM)
ANY_SPEC = pl.BlockSpec(memory_space=pl.ANY)
PARAMS = pltpu.CompilerParams(vmem_limit_bytes=VMEM_LIMIT)
AXES = ("depth", "lat")


def split_store(buffer, slot_ref):
    for offset in range(3):
        for part in range(2):
            block = buffer[offset, part]
            high = block.astype(jnp.bfloat16)
            low = (block - high.astype(jnp.float32)).astype(jnp.bfloat16)
            rows = slice(offset * TILE, (offset + 1) * TILE)
            slot_ref[rows, part * TILE : (part + 1) * TILE] = high
            slot_ref[rows, (2 + part) * TILE : (3 + part) * TILE] = low


BUFFERS = 4


def pipelined(units, start, sample, slot_of, buffers, sems):
    for ahead in range(BUFFERS - 1):

        @pl.when(ahead < units)
        def _():
            start(ahead, buffers.at[ahead], sems.at[ahead])

    def body(unit, _):
        place = lax.rem(unit, BUFFERS)
        later = lax.rem(unit + BUFFERS - 1, BUFFERS)

        @pl.when(unit + BUFFERS - 1 < units)
        def _():
            start(unit + BUFFERS - 1, buffers.at[later], sems.at[later])

        pltpu.make_async_copy(sample, buffers.at[place], sems.at[place]).wait()
        split_store(buffers.at[place], slot_of(unit))
        return 0

    lax.fori_loop(0, units, body, 0)


def chip_body(ids, source, *refs, mine):
    packed, buffers, sems = refs[-3:]
    core = ids[1]
    first = 2 * core if mine else 2 * (1 - core)
    count = OWN + HALO

    def start(unit, buffer, sem):
        block = source.at[unit // count, lax.rem(unit, count) + core]
        pltpu.make_async_copy(block, buffer, sem).start()

    def slot_of(unit):
        return packed.at[first + unit // count, lax.rem(unit, count) + HALO * (1 - core)]

    pipelined(2 * count, start, source.at[0, 0], slot_of, buffers, sems)


def pick(number, values):
    result = jnp.int32(values[0])
    for index, value in enumerate(values[1:], 1):
        result = jnp.where(number == index, value, result)
    return result


def halo_body(ids, straight, cross, *refs, rows, slots):
    packed, buffers, sems = refs[-3:]
    row, core = ids[0], ids[1]
    units = len(slots[0])
    first = units // 2

    def start(unit, buffer, sem):
        @pl.when(unit < first)
        def _():
            pltpu.make_async_copy(straight.at[unit], buffer, sem).start()

        @pl.when(unit >= first)
        def _():
            pltpu.make_async_copy(cross.at[unit - first], buffer, sem).start()

    def slot_of(unit):
        number = unit + units * core
        return packed.at[
            pick(number, [layer for side in slots for layer, _ in side]),
            pick(number, [slot for side in slots for _, slot in side]),
        ]

    @pl.when((row >= rows[0]) & (row < rows[1]))
    def _():
        pipelined(units, start, straight.at[0], slot_of, buffers, sems)


PACKED = (GROUP, SLOTS, 3 * TILE, 4 * TILE)
PACK_SCRATCH = [
    pltpu.VMEM((BUFFERS, 3, 2, TILE, TILE), jnp.float32),
    pltpu.SemaphoreType.DMA((BUFFERS,)),
]


def pack_chip(ids, source, packed, mine):
    extra = () if packed is None else (packed,)
    return pl.pallas_call(
        functools.partial(chip_body, mine=mine),
        in_specs=[SMEM_SPEC, ANY_SPEC] + [VMEM_SPEC] * len(extra),
        out_specs=VMEM_SPEC,
        out_shape=jax.ShapeDtypeStruct(PACKED, jnp.bfloat16),
        scratch_shapes=PACK_SCRATCH,
        input_output_aliases={2: 0} if extra else {},
        compiler_params=PARAMS,
        name="pack_mine" if mine else "pack_partner",
    )(ids, pltpu.with_memory_space_constraint(source, pltpu.HBM) if mine else source, *extra)


def pack_halo(ids, sources, packed, rows, slots, name):
    return pl.pallas_call(
        functools.partial(halo_body, rows=rows, slots=slots),
        in_specs=[SMEM_SPEC, ANY_SPEC, ANY_SPEC, VMEM_SPEC],
        out_specs=VMEM_SPEC,
        out_shape=jax.ShapeDtypeStruct(PACKED, jnp.bfloat16),
        scratch_shapes=PACK_SCRATCH,
        input_output_aliases={3: 0},
        compiler_params=PARAMS,
        name=name,
    )(ids, *sources, packed)


def cut_body(ids, mine, other, straight, cross, sems, *, parts):
    row = ids[0]
    for begin_row, end_row, runs in parts:
        for side in range(2):

            @pl.when((row >= begin_row) & (row < end_row) & (ids[1] == side))
            def _():
                copies = []
                for out, entries in zip((straight, cross), runs[side]):
                    place = 0
                    for layer, begin, end in entries:
                        source = mine if layer // 2 == side else other
                        target = out.at[place : place + end - begin]
                        copies.append(
                            pltpu.make_async_copy(
                                source.at[layer % 2, begin:end], target, sems.at[len(copies)]
                            )
                        )
                        place += end - begin
                for copy in copies:
                    copy.start()
                for copy in copies:
                    copy.wait()


def cut(ids, mine, other, parts, name):
    count = sum(end - begin for _, begin, end in parts[0][2][0][0])
    return pl.pallas_call(
        functools.partial(cut_body, parts=parts),
        in_specs=[SMEM_SPEC, ANY_SPEC, ANY_SPEC],
        out_specs=[ANY_SPEC] * 2,
        out_shape=[pltpu.VMEM((count, 3, 2, TILE, TILE), jnp.float32)] * 2,
        scratch_shapes=[pltpu.SemaphoreType.DMA((6,))],
        compiler_params=PARAMS,
        name=name,
    )(ids, pltpu.with_memory_space_constraint(mine, pltpu.HBM), other)


ROWS = 20


def rows_body(ids, cells, layers, rhs, couple, rows):
    strip = rhs.shape[-1]
    shot = lax.broadcasted_iota(jnp.int32, (8, strip), 0)
    position = lax.broadcasted_iota(jnp.int32, (8, strip), 1) + ids[2] * strip
    target = jnp.full((8, strip), -1, jnp.int32)
    depth = jnp.full((8, strip), -1, jnp.int32)
    for index in range(8):
        target = jnp.where(shot == index, cells[index], target)
        depth = jnp.where(shot == index, layers[index], depth)
    here = target == position
    for layer in range(2):
        hit = here & (depth == ids[3] * 2 + layer)
        rows[layer, 0:8] = rhs[0, layer] + jnp.where(hit, 4.0, 0.0)
        rows[layer, 8:16] = rhs[1, layer]
        for way in range(2):
            for part in range(2):
                spot = 16 + 2 * way + part
                rows[layer, spot : spot + 1] = couple[way, part, layer : layer + 1]


def edge_body(ids, rows, other, edge):
    for side in range(2):

        @pl.when(ids[1] == side)
        def _():
            mine, partner = slice(2 * side, 2 * side + 2), slice(2 - 2 * side, 4 - 2 * side)
            where = slice(HALF, 2 * HALF) if side == 0 else slice(0, HALF)
            edge[mine] = rows[:, :, where]
            edge[partner] = other[:, :, where]


def window_body(ids, rows, other, beside, window):
    for side in range(2):

        @pl.when(ids[1] == side)
        def _():
            mine, partner = slice(2 * side, 2 * side + 2), slice(2 - 2 * side, 4 - 2 * side)
            chip = slice(HALF, WINDOW) if side == 0 else slice(0, 2 * HALF)
            rest = slice(0, HALF) if side == 0 else slice(2 * HALF, WINDOW)
            window[mine, :, chip] = rows[...]
            window[partner, :, chip] = other[...]
            window[:, :, rest] = beside[...]


def small_call(body, smem, arrays, shape, name):
    return pl.pallas_call(
        body,
        in_specs=[SMEM_SPEC] * len(smem) + [VMEM_SPEC] * len(arrays),
        out_specs=VMEM_SPEC,
        out_shape=jax.ShapeDtypeStruct(shape, jnp.float32),
        compiler_params=PARAMS,
        name=name,
    )(*smem, *arrays)


def store_parts(parts_ref, where, value):
    high = value.astype(jnp.bfloat16)
    parts_ref[0:16, where] = high
    parts_ref[16:32, where] = (value - high.astype(jnp.float32)).astype(jnp.bfloat16)


def scaled(coef_real, coef_imag, value):
    real, imag = value[0:8], value[8:16]
    return jnp.concatenate(
        [coef_real * real - coef_imag * imag, coef_real * imag + coef_imag * real], axis=0
    )


def tile_product(parts_ref, packed, layer, spot):
    product = jnp.dot(
        parts_ref[:, spot * TILE : (spot + 3) * TILE],
        packed[layer, spot],
        preferred_element_type=jnp.float32,
    )
    rows = product[0:16] + product[16:32]
    both = rows[:, 0 : 2 * TILE] + rows[:, 2 * TILE : 4 * TILE]
    real, imag = both[0:8], both[8:16]
    return jnp.concatenate(
        [real[:, 0:TILE] - imag[:, TILE:], real[:, TILE:] + imag[:, 0:TILE]], axis=0
    )


def lanes(start, stop):
    return slice(start * TILE, stop * TILE)


def down_body(ids, low, mid, high, window, packed, _, out, waves, parts, *, turn):
    @pl.when(ids[0] == turn)
    def _():
        for layer in range(GROUP):
            reach = HALO - layer
            if layer == 0:
                pieces = [(lanes(0, 4), low[...]), (lanes(4, 8), mid[...]), (lanes(8, 12), high[...])]
            else:
                begin, end = HALO - reach - 1, HALO + OWN + reach + 1
                pieces = [(lanes(begin + 1, end + 1), waves[layer - 1, :, lanes(begin, end)])]
            for where, value in pieces:
                forcing = window[layer, 0:16, where]
                coef_real = window[layer, 16:17, where]
                coef_imag = window[layer, 17:18, where]
                store_parts(parts, where, forcing + scaled(coef_real, coef_imag, value))
            for spot in range(HALO - reach, HALO + OWN + reach):
                waves[layer, :, lanes(spot, spot + 1)] = tile_product(parts, packed, layer, spot)
        out[...] = waves[GROUP - 1, :, lanes(HALO, HALO + OWN)]


def pair_body(ids, low, mid, high, window, packed, _, *refs, turn, first):
    outs, waves, parts = refs[:-2], refs[-2], refs[-1]

    @pl.when(ids[0] == turn)
    def _():
        for layer in (first, first + 1):
            if layer == 0:
                pieces = [
                    (lanes(2, 4), low[:, lanes(2, 4)]),
                    (lanes(4, 8), mid[...]),
                    (lanes(8, 10), high[:, lanes(0, 2)]),
                ]
            elif layer == 2:
                waves[1, :, lanes(1, 3)] = low[...]
                waves[1, :, lanes(7, 9)] = high[...]
                pieces = [(lanes(2, 10), waves[1, :, lanes(1, 9)])]
            else:
                pieces = [(lanes(3, 9), waves[layer - 1, :, lanes(2, 8)])]
            for where, value in pieces:
                forcing = window[layer, 0:16, where]
                coef_real = window[layer, 16:17, where]
                coef_imag = window[layer, 17:18, where]
                store_parts(parts, where, forcing + scaled(coef_real, coef_imag, value))
            reach = first + 1 - layer
            for spot in range(HALO - reach, HALO + OWN + reach):
                waves[layer, :, lanes(spot, spot + 1)] = tile_product(parts, packed, layer, spot)
        if first:
            outs[0][...] = waves[3, :, lanes(HALO, HALO + OWN)]
        else:
            outs[0][...] = waves[1, :, lanes(HALO, HALO + 2)]
            outs[1][...] = waves[1, :, lanes(HALO + 2, HALO + OWN)]


def up_body(ids, low, mid, high, window, packed, waves, left, right, _, out, field, parts, span, *, turn):
    @pl.when(ids[0] == turn)
    def _():
        for layer in reversed(range(GROUP)):
            reach = layer
            if layer == GROUP - 1:
                pieces = [(lanes(0, 4), low[...]), (lanes(4, 8), mid[...]), (lanes(8, 12), high[...])]
            else:
                begin, end = HALO - reach - 1, HALO + OWN + reach + 1
                pieces = [(lanes(begin + 1, end + 1), span[:, lanes(begin, end)])]
            for where, value in pieces:
                coef_real = window[layer, 18:19, where]
                coef_imag = window[layer, 19:20, where]
                store_parts(parts, where, scaled(coef_real, coef_imag, value))
            for spot in range(HALO - reach, HALO + OWN + reach):
                if layer >= 2 and spot < HALO:
                    wave = left[layer - 2, :, lanes(spot + 1, spot + 2)]
                elif layer >= 2 and spot >= HALO + OWN:
                    wave = right[layer - 2, :, lanes(spot - HALO - OWN, spot - HALO - OWN + 1)]
                else:
                    wave = waves[layer, :, lanes(spot, spot + 1)]
                span[:, lanes(spot, spot + 1)] = wave + tile_product(parts, packed, layer, spot)
            field[layer] = span[:, lanes(HALO, HALO + OWN)]
        out[...] = span[:, lanes(HALO, HALO + OWN)]


PARTS = pltpu.VMEM((32, WINDOW), jnp.bfloat16)


def down_step(ids, received, window, packed, waves, turn):
    return pl.pallas_call(
        functools.partial(down_body, turn=turn),
        in_specs=[SMEM_SPEC] + [VMEM_SPEC] * 6,
        out_specs=(VMEM_SPEC, VMEM_SPEC),
        out_shape=(
            jax.ShapeDtypeStruct((16, HALF), jnp.float32),
            jax.ShapeDtypeStruct((GROUP, 16, SPAN), jnp.float32),
        ),
        scratch_shapes=[PARTS],
        input_output_aliases={6: 1},
        compiler_params=PARAMS,
        name=f"down_{turn}",
    )(ids, *received, window, packed, waves)


def pair_step(ids, low, mid, high, window, packed, waves, turn, first):
    widths = (HALF,) if first else (2 * TILE, 2 * TILE)
    return pl.pallas_call(
        functools.partial(pair_body, turn=turn, first=first),
        in_specs=[SMEM_SPEC] + [VMEM_SPEC] * 6,
        out_specs=(VMEM_SPEC,) * (len(widths) + 1),
        out_shape=tuple(jax.ShapeDtypeStruct((16, width), jnp.float32) for width in widths)
        + (jax.ShapeDtypeStruct((GROUP, 16, SPAN), jnp.float32),),
        scratch_shapes=[PARTS],
        input_output_aliases={6: len(widths)},
        compiler_params=PARAMS,
        name=f"pair_{turn}_{first}",
    )(ids, low, mid, high, window, packed, waves)


def up_step(ids, received, window, packed, waves, left, right, field, turn):
    return pl.pallas_call(
        functools.partial(up_body, turn=turn),
        in_specs=[SMEM_SPEC] + [VMEM_SPEC] * 9,
        out_specs=(VMEM_SPEC, VMEM_SPEC),
        out_shape=(
            jax.ShapeDtypeStruct((16, HALF), jnp.float32),
            jax.ShapeDtypeStruct((GROUP, 16, HALF), jnp.float32),
        ),
        scratch_shapes=[PARTS, pltpu.VMEM((16, SPAN), jnp.float32)],
        input_output_aliases={9: 1},
        compiler_params=PARAMS,
        name=f"up_{turn}",
    )(ids, *received, window, packed, waves, left, right, field)


def give_body(ids, waves, field, give):
    own = slice(HALO * TILE, (HALO + OWN) * TILE)
    for side in range(2):

        @pl.when(ids[1] == side)
        def _():
            partner = slice(2 - 2 * side, 4 - 2 * side)
            give[0] = waves[partner, :, own]
            give[1] = field[partner]


def join_body(ids, waves, field, taken, out_waves, out_field):
    for side in range(2):

        @pl.when(ids[1] == side)
        def _():
            mine = slice(HALF * side, HALF * (side + 1))
            partner = slice(HALF * (1 - side), HALF * (2 - side))
            for layer in range(2):
                for part in range(2):
                    rows = slice(8 * part, 8 * (part + 1))
                    own = slice(HALO * TILE, (HALO + OWN) * TILE)
                    out_waves[part, layer, :, mine] = waves[2 * side + layer, rows, own]
                    out_field[part, layer, :, mine] = field[2 * side + layer, rows]
                    out_waves[part, layer, :, partner] = taken[0, layer, rows]
                    out_field[part, layer, :, partner] = taken[1, layer, rows]


def join(ids, waves, field, taken, shape):
    return pl.pallas_call(
        join_body,
        in_specs=[SMEM_SPEC] + [VMEM_SPEC] * 3,
        out_specs=(VMEM_SPEC,) * 2,
        out_shape=(jax.ShapeDtypeStruct(shape, jnp.float32),) * 2,
        compiler_params=PARAMS,
        name="join",
    )(ids, waves, field, taken)


PAIR_ROWS = 2
LATE_ROWS = 5
FIRST_RUNS = (
    (((0, 7, 8),), ((0, 0, 1),)),
    (((2, 0, 1),), ((2, 7, 8),)),
)
FIRST_SLOTS = (((0, 2), (2, 2)), ((2, 7), (0, 7)))
DOWN_RUNS = (
    (((0, 5, 8),), ((0, 0, 3),)),
    (((1, 0, 2), (2, 0, 1)), ((1, 6, 8), (2, 7, 8))),
)
DOWN_SLOTS = (
    ((0, 0), (0, 1), (0, 2), (1, 1), (1, 2), (2, 2)),
    ((1, 7), (1, 8), (2, 7), (0, 7), (0, 8), (0, 9)),
)
EARLY_RUNS = (
    (((3, 7, 8), (2, 6, 7)), ((3, 0, 1), (2, 1, 2))),
    (((3, 1, 3),), ((3, 5, 7),)),
)
EARLY_SLOTS = (
    ((3, 2), (2, 1), (3, 0), (3, 1)),
    ((3, 8), (3, 9), (3, 7), (2, 8)),
)
EXTRA_RUNS = (
    (((1, 7, 8), (2, 6, 7)), ((1, 0, 1), (2, 1, 2))),
    (((3, 1, 3),), ((3, 5, 7),)),
)
EXTRA_SLOTS = (
    ((1, 2), (2, 1), (3, 0), (3, 1)),
    ((3, 8), (3, 9), (1, 7), (2, 8)),
)


def gated(value, *others):
    return lax.optimization_barrier((value, *others))[0]


def shards(rhs_field, src_cell, src_layer, factor, couple):
    layer_total, shot_count, strip_cells = rhs_field.shape[1:]
    depth_count, lat_count = lax.axis_size("depth"), lax.axis_size("lat")
    depth_pos, lat_pos = lax.axis_index("depth"), lax.axis_index("lat")
    core = lax.rem(depth_pos, 2)
    first_core = core == 0
    chip_rows = depth_count // 2
    halves = 2 * lat_count
    everyone = range(chip_rows)
    ids = jnp.stack([depth_pos // 2, core, lat_pos, depth_pos]).astype(jnp.int32)

    def device(row, half):
        return (2 * row + half % 2) * lat_count + half // 2

    def at(depth, lat):
        return depth * lat_count + lat

    def hop(value, rows, step, shift):
        pairs = [
            (device(row, half), device(row + step, half + shift))
            for row in rows
            if 0 <= row + step < chip_rows
            for half in range(halves)
            if 0 <= half + shift < halves
        ]
        return lax.ppermute(value, AXES, pairs)

    partner = [(at(d, l), at(d ^ 1, l)) for d in range(depth_count) for l in range(lat_count)]

    def beside_pairs(rows, same):
        pairs = []
        for row in rows:
            for side in range(2):
                shift = 1 if (side == 0) == same else -1
                target = side if same else 1 - side
                pairs += [
                    (at(2 * row + side, l), at(2 * row + target, l + shift))
                    for l in range(lat_count)
                    if 0 <= l + shift < lat_count
                ]
        return pairs

    def send_halo(ids, other, parts, name):
        straight, cross = cut(ids, factor, other, parts, name)
        rows = [row for begin, end, _ in parts for row in range(begin, end)]
        return straight, (
            lax.ppermute(straight, AXES, beside_pairs(rows, True)),
            lax.ppermute(cross, AXES, beside_pairs(rows, False)),
        )

    first_cut, first_halo = send_halo(ids, factor, ((0, PAIR_ROWS, FIRST_RUNS),), "cut_first")
    other = lax.ppermute(gated(factor, first_cut), AXES, partner)

    rows = small_call(
        rows_body, (ids, src_cell, src_layer), (rhs_field, couple), (layer_total, ROWS, strip_cells), "rows"
    )
    rows_other = lax.ppermute(rows, AXES, partner)
    edge = small_call(edge_body, (ids,), (rows, rows_other), (GROUP, ROWS, HALF), "edge")
    packed = pack_chip(gated(ids, rows), factor, None, True)
    other, packed = lax.optimization_barrier((other, packed, edge))[:2]
    beside = lax.ppermute(edge, AXES, beside_pairs(everyone, True))
    window = small_call(
        window_body, (ids,), (rows, rows_other, beside), (GROUP, ROWS, WINDOW), "window"
    )
    down_parts = ((PAIR_ROWS, chip_rows, DOWN_RUNS),)
    early_parts = ((LATE_ROWS, chip_rows, EARLY_RUNS), (0, PAIR_ROWS, EXTRA_RUNS))
    late_parts = ((0, LATE_ROWS, EARLY_RUNS),)
    _, halo = send_halo(gated(ids, beside), other, down_parts, "cut_down")
    packed = pack_chip(ids, other, packed, False)
    packed = pack_halo(
        gated(ids, window), first_halo, packed, (0, PAIR_ROWS), FIRST_SLOTS, "halo_first"
    )

    zero_half = jnp.zeros((2 * shot_count, HALF), jnp.float32)
    waves = jnp.zeros((GROUP, 2 * shot_count, SPAN), jnp.float32)
    field = jnp.zeros((GROUP, 2 * shot_count, HALF), jnp.float32)

    received = (zero_half,) * 3
    for turn in everyone:
        if turn < PAIR_ROWS:
            left_edge, right_edge, waves = pair_step(
                ids, *received, window, packed, waves, turn, 0
            )
            pairs = range(PAIR_ROWS)
            low, high = hop(right_edge, pairs, 0, 1), hop(left_edge, pairs, 0, -1)
            out, waves = pair_step(ids, low, left_edge, high, window, packed, waves, turn, 2)
            if turn + 1 == PAIR_ROWS:
                down_rows = (PAIR_ROWS, chip_rows)
                packed = pack_halo(gated(ids, out), halo, packed, down_rows, DOWN_SLOTS, "halo_down")
                _, halo = send_halo(gated(ids, out, *halo), other, early_parts, "cut_early")
                out, packed = lax.optimization_barrier((out, packed))
        else:
            out, waves = down_step(ids, received, window, packed, waves, turn)
            if turn + 1 == LATE_ROWS:
                late_ids = gated(ids, out)
                early_rows, first_rows = (LATE_ROWS, chip_rows), (0, PAIR_ROWS)
                packed = pack_halo(late_ids, halo, packed, early_rows, EARLY_SLOTS, "halo_early")
                packed = pack_halo(late_ids, halo, packed, first_rows, EXTRA_SLOTS, "halo_extra")
                out, packed = lax.optimization_barrier((out, packed))
            if turn == LATE_ROWS:
                _, halo = send_halo(gated(ids, out), other, late_parts, "cut_late")
        if turn + 1 < chip_rows:
            group = range(turn % 3, chip_rows, 3)
            received = (hop(out, group, 1, 1), hop(out, group, 1, 0), hop(out, group, 1, -1))

    deep = waves[2:, :, HALO * TILE : (HALO + OWN) * TILE]
    left, right = hop(deep, everyone, 0, 1), hop(deep, everyone, 0, -1)
    received = (zero_half,) * 3
    for turn in reversed(everyone):
        out, field = up_step(ids, received, window, packed, waves, left, right, field, turn)
        if turn == LATE_ROWS:
            packed = pack_halo(gated(ids, out), halo, packed, (0, LATE_ROWS), EARLY_SLOTS, "halo_late")
            out, packed = lax.optimization_barrier((out, packed))
        if turn:
            group = range(turn % 3, chip_rows, 3)
            received = (hop(out, group, -1, 1), hop(out, group, -1, 0), hop(out, group, -1, -1))

    shape = (2, layer_total, 2 * shot_count, HALF)
    waves = gated(waves, field)
    give = small_call(give_body, (ids,), (waves, field), shape, "give")
    taken = lax.ppermute(give, AXES, partner)
    return join(ids, waves, field, taken, rhs_field.shape)


def solution(mesh):
    placed = (
        P(None, "depth", None, "lat"),
        P(),
        P(),
        P("depth", "lat", None, None, None, None),
        P(None, None, "depth", "lat"),
    )
    return jax.shard_map(
        shards,
        mesh=mesh,
        in_specs=placed,
        out_specs=(P(None, "depth", None, "lat"), P(None, "depth", None, "lat")),
        check_vma=False,
    )
```

```python
import functools

import jax
import jax.numpy as jnp
from jax import lax
from jax.experimental import pallas as pl
from jax.experimental.pallas import tpu as pltpu
from jax.sharding import PartitionSpec as P

TILE = 128
GROUP = 4
OWN = 4
HALO = 3
SLOTS = OWN + 2 * HALO
WINDOW = (OWN + 2 * (HALO + 1)) * TILE
SPAN = SLOTS * TILE
HALF = OWN * TILE
VMEM_LIMIT = 10 << 20

VMEM_SPEC = pl.BlockSpec(memory_space=pltpu.VMEM)
SMEM_SPEC = pl.BlockSpec(memory_space=pltpu.SMEM)
ANY_SPEC = pl.BlockSpec(memory_space=pl.ANY)
PARAMS = pltpu.CompilerParams(vmem_limit_bytes=VMEM_LIMIT)
BRIEF = pl.CostEstimate(flops=1, transcendentals=0, bytes_accessed=1)
AXES = ("depth", "lat")


def split_store(buffer, slot_ref):
    for offset in range(3):
        for part in range(2):
            block = buffer[offset, part]
            high = block.astype(jnp.bfloat16)
            low = (block - high.astype(jnp.float32)).astype(jnp.bfloat16)
            rows = slice(offset * TILE, (offset + 1) * TILE)
            slot_ref[rows, part * TILE : (part + 1) * TILE] = high
            slot_ref[rows, (2 + part) * TILE : (3 + part) * TILE] = low


BUFFERS = 4


def pipelined(units, start, sample, slot_of, buffers, sems):
    for ahead in range(BUFFERS - 1):

        @pl.when(ahead < units)
        def _():
            start(ahead, buffers.at[ahead], sems.at[ahead])

    def body(unit, _):
        place = lax.rem(unit, BUFFERS)
        later = lax.rem(unit + BUFFERS - 1, BUFFERS)

        @pl.when(unit + BUFFERS - 1 < units)
        def _():
            start(unit + BUFFERS - 1, buffers.at[later], sems.at[later])

        pltpu.make_async_copy(sample, buffers.at[place], sems.at[place]).wait()
        split_store(buffers.at[place], slot_of(unit))
        return 0

    lax.fori_loop(0, units, body, 0)


def chip_body(ids, source, *refs, mine):
    packed, buffers, sems = refs[-3:]
    core = ids[1]
    first = 2 * core if mine else 2 * (1 - core)
    count = OWN + HALO

    def start(unit, buffer, sem):
        block = source.at[unit // count, lax.rem(unit, count) + core]
        pltpu.make_async_copy(block, buffer, sem).start()

    def slot_of(unit):
        return packed.at[first + unit // count, lax.rem(unit, count) + HALO * (1 - core)]

    pipelined(2 * count, start, source.at[0, 0], slot_of, buffers, sems)


def pick(number, values):
    result = jnp.int32(values[0])
    for index, value in enumerate(values[1:], 1):
        result = jnp.where(number == index, value, result)
    return result


def halo_body(ids, straight, cross, *refs, rows, slots, split):
    packed, buffers, sems = refs[-3:]
    row, core = ids[0], ids[1]
    units = len(slots[0])
    first = units // 2

    def start(unit, buffer, sem):
        by_straight = unit < first if split else core == 0
        place = lax.rem(unit, first) if split else unit

        @pl.when(by_straight)
        def _():
            pltpu.make_async_copy(straight.at[place], buffer, sem).start()

        @pl.when(jnp.logical_not(by_straight))
        def _():
            pltpu.make_async_copy(cross.at[place], buffer, sem).start()

    def slot_of(unit):
        number = unit + units * core
        return packed.at[
            pick(number, [layer for side in slots for layer, _ in side]),
            pick(number, [slot for side in slots for _, slot in side]),
        ]

    @pl.when((row >= rows[0]) & (row < rows[1]))
    def _():
        pipelined(units, start, straight.at[0], slot_of, buffers, sems)


PACKED = (GROUP, SLOTS, 3 * TILE, 4 * TILE)
PACK_SCRATCH = [
    pltpu.VMEM((BUFFERS, 3, 2, TILE, TILE), jnp.float32),
    pltpu.SemaphoreType.DMA((BUFFERS,)),
]


def pack_chip(ids, source, packed, mine):
    extra = () if packed is None else (packed,)
    return pl.pallas_call(
        functools.partial(chip_body, mine=mine),
        in_specs=[SMEM_SPEC, ANY_SPEC] + [VMEM_SPEC] * len(extra),
        out_specs=VMEM_SPEC,
        out_shape=jax.ShapeDtypeStruct(PACKED, jnp.bfloat16),
        scratch_shapes=PACK_SCRATCH,
        input_output_aliases={2: 0} if extra else {},
        compiler_params=PARAMS,
        cost_estimate=BRIEF,
        name="pack_mine" if mine else "pack_partner",
    )(ids, pltpu.with_memory_space_constraint(source, pltpu.HBM) if mine else source, *extra)


def pack_halo(ids, sources, packed, rows, slots, name, split=True):
    return pl.pallas_call(
        functools.partial(halo_body, rows=rows, slots=slots, split=split),
        in_specs=[SMEM_SPEC, ANY_SPEC, ANY_SPEC, VMEM_SPEC],
        out_specs=VMEM_SPEC,
        out_shape=jax.ShapeDtypeStruct(PACKED, jnp.bfloat16),
        scratch_shapes=PACK_SCRATCH,
        input_output_aliases={3: 0},
        compiler_params=PARAMS,
        cost_estimate=BRIEF,
        name=name,
    )(ids, *sources, packed)


def cut_body(ids, mine, other, straight, cross, sems, *, parts):
    row = ids[0]
    for begin_row, end_row, runs in parts:
        for side in range(2):

            @pl.when((row >= begin_row) & (row < end_row) & (ids[1] == side))
            def _():
                copies = []
                for out, entries in zip((straight, cross), runs[side]):
                    place = 0
                    for layer, begin, end in entries:
                        source = mine if layer // 2 == side else other
                        target = out.at[place : place + end - begin]
                        copies.append(
                            pltpu.make_async_copy(
                                source.at[layer % 2, begin:end], target, sems.at[len(copies)]
                            )
                        )
                        place += end - begin
                for copy in copies:
                    copy.start()
                for copy in copies:
                    copy.wait()


def cut(ids, mine, other, parts, name):
    count = sum(end - begin for _, begin, end in parts[0][2][0][0])
    return pl.pallas_call(
        functools.partial(cut_body, parts=parts),
        in_specs=[SMEM_SPEC, ANY_SPEC, ANY_SPEC],
        out_specs=[ANY_SPEC] * 2,
        out_shape=[pltpu.VMEM((count, 3, 2, TILE, TILE), jnp.float32)] * 2,
        scratch_shapes=[pltpu.SemaphoreType.DMA((6,))],
        compiler_params=PARAMS,
        cost_estimate=BRIEF,
        name=name,
    )(ids, pltpu.with_memory_space_constraint(mine, pltpu.HBM), other)


ROWS = 20


def rows_body(ids, cells, layers, rhs, couple, rows):
    strip = rhs.shape[-1]
    shot = lax.broadcasted_iota(jnp.int32, (8, strip), 0)
    position = lax.broadcasted_iota(jnp.int32, (8, strip), 1) + ids[2] * strip
    target = jnp.full((8, strip), -1, jnp.int32)
    depth = jnp.full((8, strip), -1, jnp.int32)
    for index in range(8):
        target = jnp.where(shot == index, cells[index], target)
        depth = jnp.where(shot == index, layers[index], depth)
    here = target == position
    for layer in range(2):
        hit = here & (depth == ids[3] * 2 + layer)
        rows[layer, 0:8] = rhs[0, layer] + jnp.where(hit, 4.0, 0.0)
        rows[layer, 8:16] = rhs[1, layer]
        for way in range(2):
            for part in range(2):
                spot = 16 + 2 * way + part
                rows[layer, spot : spot + 1] = couple[way, part, layer : layer + 1]


def edge_body(ids, rows, other, edge):
    for side in range(2):

        @pl.when(ids[1] == side)
        def _():
            mine, partner = slice(2 * side, 2 * side + 2), slice(2 - 2 * side, 4 - 2 * side)
            where = slice(HALF, 2 * HALF) if side == 0 else slice(0, HALF)
            edge[mine] = rows[:, :, where]
            edge[partner] = other[:, :, where]


def window_body(ids, rows, other, beside, window):
    for side in range(2):

        @pl.when(ids[1] == side)
        def _():
            mine, partner = slice(2 * side, 2 * side + 2), slice(2 - 2 * side, 4 - 2 * side)
            chip = slice(HALF, WINDOW) if side == 0 else slice(0, 2 * HALF)
            rest = slice(0, HALF) if side == 0 else slice(2 * HALF, WINDOW)
            window[mine, :, chip] = rows[...]
            window[partner, :, chip] = other[...]
            window[:, :, rest] = beside[...]


def small_call(body, smem, arrays, shape, name):
    return pl.pallas_call(
        body,
        in_specs=[SMEM_SPEC] * len(smem) + [VMEM_SPEC] * len(arrays),
        out_specs=VMEM_SPEC,
        out_shape=jax.ShapeDtypeStruct(shape, jnp.float32),
        compiler_params=PARAMS,
        cost_estimate=BRIEF,
        name=name,
    )(*smem, *arrays)


def store_parts(parts_ref, where, value):
    high = value.astype(jnp.bfloat16)
    parts_ref[0:16, where] = high
    parts_ref[16:32, where] = (value - high.astype(jnp.float32)).astype(jnp.bfloat16)


def scaled(coef_real, coef_imag, value):
    real, imag = value[0:8], value[8:16]
    return jnp.concatenate(
        [coef_real * real - coef_imag * imag, coef_real * imag + coef_imag * real], axis=0
    )


def tile_product(parts_ref, packed, layer, spot):
    product = jnp.dot(
        parts_ref[:, spot * TILE : (spot + 3) * TILE],
        packed[layer, spot],
        preferred_element_type=jnp.float32,
    )
    rows = product[0:16] + product[16:32]
    both = rows[:, 0 : 2 * TILE] + rows[:, 2 * TILE : 4 * TILE]
    real, imag = both[0:8], both[8:16]
    return jnp.concatenate(
        [real[:, 0:TILE] - imag[:, TILE:], real[:, TILE:] + imag[:, 0:TILE]], axis=0
    )


def lanes(start, stop):
    return slice(start * TILE, stop * TILE)


def down_body(ids, low, mid, high, window, packed, _, out, waves, parts, *, turn):
    @pl.when(ids[0] == turn)
    def _():
        for layer in range(GROUP):
            reach = HALO - layer
            if layer == 0:
                pieces = [(lanes(0, 4), low[...]), (lanes(4, 8), mid[...]), (lanes(8, 12), high[...])]
            else:
                begin, end = HALO - reach - 1, HALO + OWN + reach + 1
                pieces = [(lanes(begin + 1, end + 1), waves[layer - 1, :, lanes(begin, end)])]
            for where, value in pieces:
                forcing = window[layer, 0:16, where]
                coef_real = window[layer, 16:17, where]
                coef_imag = window[layer, 17:18, where]
                store_parts(parts, where, forcing + scaled(coef_real, coef_imag, value))
            for spot in range(HALO - reach, HALO + OWN + reach):
                waves[layer, :, lanes(spot, spot + 1)] = tile_product(parts, packed, layer, spot)
        out[...] = waves[GROUP - 1, :, lanes(HALO, HALO + OWN)]


def pair_body(ids, low, mid, high, window, packed, _, *refs, turn, first):
    outs, waves, parts = refs[:-2], refs[-2], refs[-1]

    @pl.when(ids[0] == turn)
    def _():
        for layer in (first, first + 1):
            if layer == 0:
                pieces = [
                    (lanes(2, 4), low[:, lanes(2, 4)]),
                    (lanes(4, 8), mid[...]),
                    (lanes(8, 10), high[:, lanes(0, 2)]),
                ]
            elif layer == 2:
                waves[1, :, lanes(1, 3)] = low[...]
                waves[1, :, lanes(7, 9)] = high[...]
                pieces = [(lanes(2, 10), waves[1, :, lanes(1, 9)])]
            else:
                pieces = [(lanes(3, 9), waves[layer - 1, :, lanes(2, 8)])]
            for where, value in pieces:
                forcing = window[layer, 0:16, where]
                coef_real = window[layer, 16:17, where]
                coef_imag = window[layer, 17:18, where]
                store_parts(parts, where, forcing + scaled(coef_real, coef_imag, value))
            reach = first + 1 - layer
            for spot in range(HALO - reach, HALO + OWN + reach):
                waves[layer, :, lanes(spot, spot + 1)] = tile_product(parts, packed, layer, spot)
        if first:
            outs[0][...] = waves[3, :, lanes(HALO, HALO + OWN)]
        else:
            outs[0][...] = waves[1, :, lanes(HALO, HALO + 2)]
            outs[1][...] = waves[1, :, lanes(HALO + 2, HALO + OWN)]


def up_body(ids, low, mid, high, window, packed, waves, left, right, _, out, field, parts, span, *, turn):
    @pl.when(ids[0] == turn)
    def _():
        for layer in reversed(range(GROUP)):
            reach = layer
            if layer == GROUP - 1:
                pieces = [(lanes(0, 4), low[...]), (lanes(4, 8), mid[...]), (lanes(8, 12), high[...])]
            else:
                begin, end = HALO - reach - 1, HALO + OWN + reach + 1
                pieces = [(lanes(begin + 1, end + 1), span[:, lanes(begin, end)])]
            for where, value in pieces:
                coef_real = window[layer, 18:19, where]
                coef_imag = window[layer, 19:20, where]
                store_parts(parts, where, scaled(coef_real, coef_imag, value))
            for spot in range(HALO - reach, HALO + OWN + reach):
                if layer >= 2 and spot < HALO:
                    wave = left[layer - 2, :, lanes(spot + 1, spot + 2)]
                elif layer >= 2 and spot >= HALO + OWN:
                    wave = right[layer - 2, :, lanes(spot - HALO - OWN, spot - HALO - OWN + 1)]
                else:
                    wave = waves[layer, :, lanes(spot, spot + 1)]
                span[:, lanes(spot, spot + 1)] = wave + tile_product(parts, packed, layer, spot)
            field[layer] = span[:, lanes(HALO, HALO + OWN)]
        out[...] = span[:, lanes(HALO, HALO + OWN)]


PARTS = pltpu.VMEM((32, WINDOW), jnp.bfloat16)


def down_step(ids, received, window, packed, waves, turn):
    return pl.pallas_call(
        functools.partial(down_body, turn=turn),
        in_specs=[SMEM_SPEC] + [VMEM_SPEC] * 6,
        out_specs=(VMEM_SPEC, VMEM_SPEC),
        out_shape=(
            jax.ShapeDtypeStruct((16, HALF), jnp.float32),
            jax.ShapeDtypeStruct((GROUP, 16, SPAN), jnp.float32),
        ),
        scratch_shapes=[PARTS],
        input_output_aliases={6: 1},
        compiler_params=PARAMS,
        cost_estimate=BRIEF,
        name=f"down_{turn}",
    )(ids, *received, window, packed, waves)


def pair_step(ids, low, mid, high, window, packed, waves, turn, first):
    widths = (HALF,) if first else (2 * TILE, 2 * TILE)
    return pl.pallas_call(
        functools.partial(pair_body, turn=turn, first=first),
        in_specs=[SMEM_SPEC] + [VMEM_SPEC] * 6,
        out_specs=(VMEM_SPEC,) * (len(widths) + 1),
        out_shape=tuple(jax.ShapeDtypeStruct((16, width), jnp.float32) for width in widths)
        + (jax.ShapeDtypeStruct((GROUP, 16, SPAN), jnp.float32),),
        scratch_shapes=[PARTS],
        input_output_aliases={6: len(widths)},
        compiler_params=PARAMS,
        cost_estimate=BRIEF,
        name=f"pair_{turn}_{first}",
    )(ids, low, mid, high, window, packed, waves)


def up_step(ids, received, window, packed, waves, left, right, field, turn):
    return pl.pallas_call(
        functools.partial(up_body, turn=turn),
        in_specs=[SMEM_SPEC] + [VMEM_SPEC] * 9,
        out_specs=(VMEM_SPEC, VMEM_SPEC),
        out_shape=(
            jax.ShapeDtypeStruct((16, HALF), jnp.float32),
            jax.ShapeDtypeStruct((GROUP, 16, HALF), jnp.float32),
        ),
        scratch_shapes=[PARTS, pltpu.VMEM((16, SPAN), jnp.float32)],
        input_output_aliases={9: 1},
        compiler_params=PARAMS,
        cost_estimate=BRIEF,
        name=f"up_{turn}",
    )(ids, *received, window, packed, waves, left, right, field)


def give_body(ids, waves, field, give):
    own = slice(HALO * TILE, (HALO + OWN) * TILE)
    for side in range(2):

        @pl.when(ids[1] == side)
        def _():
            partner = slice(2 - 2 * side, 4 - 2 * side)
            give[0] = waves[partner, :, own]
            give[1] = field[partner]


def join_body(ids, waves, field, taken, out_waves, out_field):
    for side in range(2):

        @pl.when(ids[1] == side)
        def _():
            mine = slice(HALF * side, HALF * (side + 1))
            partner = slice(HALF * (1 - side), HALF * (2 - side))
            for layer in range(2):
                for part in range(2):
                    rows = slice(8 * part, 8 * (part + 1))
                    own = slice(HALO * TILE, (HALO + OWN) * TILE)
                    out_waves[part, layer, :, mine] = waves[2 * side + layer, rows, own]
                    out_field[part, layer, :, mine] = field[2 * side + layer, rows]
                    out_waves[part, layer, :, partner] = taken[0, layer, rows]
                    out_field[part, layer, :, partner] = taken[1, layer, rows]


def join(ids, waves, field, taken, shape):
    return pl.pallas_call(
        join_body,
        in_specs=[SMEM_SPEC] + [VMEM_SPEC] * 3,
        out_specs=(VMEM_SPEC,) * 2,
        out_shape=(jax.ShapeDtypeStruct(shape, jnp.float32),) * 2,
        compiler_params=PARAMS,
        cost_estimate=BRIEF,
        name="join",
    )(ids, waves, field, taken)


PAIR_ROWS = 2
LATE_ROWS = 5
FIRST_RUNS = (
    (((0, 7, 8),), ((0, 0, 1),)),
    (((2, 0, 1),), ((2, 7, 8),)),
)
FIRST_SLOTS = (((0, 2), (2, 2)), ((2, 7), (0, 7)))
DOWN_RUNS = (
    (((0, 5, 7), (1, 6, 8)), ((0, 1, 3), (1, 0, 2))),
    ((), ()),
)
DOWN_SLOTS = (
    ((0, 0), (0, 1), (1, 1), (1, 2)),
    ((0, 8), (0, 9), (1, 7), (1, 8)),
)
EARLY_RUNS = (
    (((3, 7, 8), (2, 6, 7)), ((3, 0, 1), (2, 1, 2))),
    (((3, 1, 3),), ((3, 5, 7),)),
)
EARLY_SLOTS = (
    ((3, 2), (2, 1), (3, 0), (3, 1)),
    ((3, 8), (3, 9), (3, 7), (2, 8)),
)
LAST_RUNS = ((((1, 7, 8),), ((1, 0, 1),)), ((), ()))
LAST_SLOTS = (((1, 2),), ((1, 7),))


def gated(value, *others):
    return lax.optimization_barrier((value, *others))[0]


def shards(rhs_field, src_cell, src_layer, factor, couple):
    layer_total, shot_count, strip_cells = rhs_field.shape[1:]
    depth_count, lat_count = lax.axis_size("depth"), lax.axis_size("lat")
    depth_pos, lat_pos = lax.axis_index("depth"), lax.axis_index("lat")
    core = lax.rem(depth_pos, 2)
    first_core = core == 0
    chip_rows = depth_count // 2
    halves = 2 * lat_count
    everyone = range(chip_rows)
    ids = jnp.stack([depth_pos // 2, core, lat_pos, depth_pos]).astype(jnp.int32)

    def device(row, half):
        return (2 * row + half % 2) * lat_count + half // 2

    def at(depth, lat):
        return depth * lat_count + lat

    def hop(value, rows, step, shift):
        pairs = [
            (device(row, half), device(row + step, half + shift))
            for row in rows
            if 0 <= row + step < chip_rows
            for half in range(halves)
            if 0 <= half + shift < halves
        ]
        return lax.ppermute(value, AXES, pairs)

    partner = [(at(d, l), at(d ^ 1, l)) for d in range(depth_count) for l in range(lat_count)]

    def beside_pairs(rows, same, sides=(0, 1)):
        pairs = []
        for row in rows:
            for side in sides:
                shift = 1 if (side == 0) == same else -1
                target = side if same else 1 - side
                pairs += [
                    (at(2 * row + side, l), at(2 * row + target, l + shift))
                    for l in range(lat_count)
                    if 0 <= l + shift < lat_count
                ]
        return pairs

    def send_halo(ids, other, parts, name, sides=(0, 1), after=()):
        straight, cross = cut(ids, factor, other, parts, name)
        straight, cross = lax.optimization_barrier((straight, cross, *after))[:2]
        rows = [row for begin, end, _ in parts for row in range(begin, end)]
        return straight, (
            lax.ppermute(straight, AXES, beside_pairs(rows, True, sides)),
            lax.ppermute(cross, AXES, beside_pairs(rows, False, sides)),
        )

    first_cut, first_halo = send_halo(ids, factor, ((0, chip_rows, FIRST_RUNS),), "cut_first")
    down_parts = ((PAIR_ROWS, chip_rows, DOWN_RUNS),)
    early_parts = ((LATE_ROWS, chip_rows, EARLY_RUNS),)
    late_parts = ((0, LATE_ROWS, EARLY_RUNS),)
    last_parts = ((0, PAIR_ROWS, LAST_RUNS),)
    other = lax.ppermute(gated(factor, first_cut), AXES, partner)

    rows = small_call(
        rows_body,
        (gated(ids, first_cut), src_cell, src_layer),
        (rhs_field, couple),
        (layer_total, ROWS, strip_cells),
        "rows",
    )
    rows_other = lax.ppermute(rows, AXES, partner)
    packed = pack_chip(gated(ids, rows), factor, None, True)
    edge = small_call(
        edge_body, (gated(ids, packed),), (rows, rows_other), (GROUP, ROWS, HALF), "edge"
    )
    packed = pack_chip(ids, other, packed, False)
    beside = lax.ppermute(edge, AXES, beside_pairs(everyone, True))
    window = small_call(
        window_body, (gated(ids, packed, *first_halo),), (rows, rows_other, beside), (GROUP, ROWS, WINDOW), "window"
    )
    _, halo = send_halo(gated(ids, rows), factor, down_parts, "cut_down", (0,), (window, *first_halo))
    packed = pack_halo(
        gated(ids, window), first_halo, packed, (0, chip_rows), FIRST_SLOTS, "halo_first"
    )

    zero_half = jnp.zeros((2 * shot_count, HALF), jnp.float32)
    waves = jnp.zeros((GROUP, 2 * shot_count, SPAN), jnp.float32)
    field = jnp.zeros((GROUP, 2 * shot_count, HALF), jnp.float32)

    received = (zero_half,) * 3
    for turn in everyone:
        if turn < PAIR_ROWS:
            left_edge, right_edge, waves = pair_step(
                ids, *received, window, packed, waves, turn, 0
            )
            pairs = range(PAIR_ROWS)
            low, high = hop(right_edge, pairs, 0, 1), hop(left_edge, pairs, 0, -1)
            out, waves = pair_step(ids, low, left_edge, high, window, packed, waves, turn, 2)
            if turn + 1 == PAIR_ROWS:
                down_rows = (PAIR_ROWS, chip_rows)
                packed = pack_halo(
                    gated(ids, out), halo, packed, down_rows, DOWN_SLOTS, "halo_down", False
                )
                _, early_halo = send_halo(gated(ids, out, *halo), other, early_parts, "cut_early")
                out, packed = lax.optimization_barrier((out, packed))
        else:
            out, waves = down_step(ids, received, window, packed, waves, turn)
            if turn == LATE_ROWS:
                late_ids, last_rows = gated(ids, out), (LATE_ROWS + 1, chip_rows)
                packed = pack_halo(late_ids, early_halo, packed, last_rows, EARLY_SLOTS, "halo_last")
                out, packed = lax.optimization_barrier((out, packed))
                _, late_halo = send_halo(gated(ids, out), other, late_parts, "cut_late")
        if turn + 1 < chip_rows:
            group = range(turn % 3, chip_rows, 3)
            received = (hop(out, group, 1, 1), hop(out, group, 1, 0), hop(out, group, 1, -1))

    deep = waves[2:, :, HALO * TILE : (HALO + OWN) * TILE]
    left, right = hop(deep, everyone, 0, 1), hop(deep, everyone, 0, -1)
    received = (zero_half,) * 3
    for turn in reversed(everyone):
        out, field = up_step(ids, received, window, packed, waves, left, right, field, turn)
        if turn == LATE_ROWS + 1:
            row = (LATE_ROWS, LATE_ROWS + 1)
            packed = pack_halo(gated(ids, out), early_halo, packed, row, EARLY_SLOTS, "halo_early")
            out, packed = lax.optimization_barrier((out, packed))
        if turn == LATE_ROWS:
            late_rows = (0, LATE_ROWS)
            packed = pack_halo(gated(ids, out), late_halo, packed, late_rows, EARLY_SLOTS, "halo_late")
            out, packed = lax.optimization_barrier((out, packed))
        if turn == LATE_ROWS - 1:
            _, last_halo = send_halo(gated(ids, out), factor, last_parts, "cut_last", (0,))
        if turn == PAIR_ROWS:
            last_rows = (0, PAIR_ROWS)
            packed = pack_halo(
                gated(ids, out), last_halo, packed, last_rows, LAST_SLOTS, "halo_extra", False
            )
            out, packed = lax.optimization_barrier((out, packed))
        if turn:
            group = range(turn % 3, chip_rows, 3)
            received = (hop(out, group, -1, 1), hop(out, group, -1, 0), hop(out, group, -1, -1))

    shape = (2, layer_total, 2 * shot_count, HALF)
    waves = gated(waves, field)
    give = small_call(give_body, (ids,), (waves, field), shape, "give")
    taken = lax.ppermute(give, AXES, partner)
    return join(ids, waves, field, taken, rhs_field.shape)


def solution(mesh):
    placed = (
        P(None, "depth", None, "lat"),
        P(),
        P(),
        P("depth", "lat", None, None, None, None),
        P(None, None, "depth", "lat"),
    )
    return jax.shard_map(
        shards,
        mesh=mesh,
        in_specs=placed,
        out_specs=(P(None, "depth", None, "lat"), P(None, "depth", None, "lat")),
        check_vma=False,
    )
```

```python
import functools

import jax
import jax.numpy as jnp
from jax import lax
from jax.experimental import pallas as pl
from jax.experimental.pallas import tpu as pltpu
from jax.sharding import PartitionSpec as P

TILE = 128
GROUP = 4
OWN = 4
HALO = 3
SLOTS = OWN + 2 * HALO
WINDOW = (OWN + 2 * (HALO + 1)) * TILE
SPAN = SLOTS * TILE
HALF = OWN * TILE
VMEM_LIMIT = 10 << 20

VMEM_SPEC = pl.BlockSpec(memory_space=pltpu.VMEM)
SMEM_SPEC = pl.BlockSpec(memory_space=pltpu.SMEM)
ANY_SPEC = pl.BlockSpec(memory_space=pl.ANY)
PARAMS = pltpu.CompilerParams(vmem_limit_bytes=VMEM_LIMIT)
BRIEF = pl.CostEstimate(flops=1, transcendentals=0, bytes_accessed=1)
AXES = ("depth", "lat")


def split_store(buffer, slot_ref):
    for offset in range(3):
        for part in range(2):
            block = buffer[offset, part]
            high = block.astype(jnp.bfloat16)
            low = (block - high.astype(jnp.float32)).astype(jnp.bfloat16)
            rows = slice(offset * TILE, (offset + 1) * TILE)
            slot_ref[rows, part * TILE : (part + 1) * TILE] = high
            slot_ref[rows, (2 + part) * TILE : (3 + part) * TILE] = low


BUFFERS = 4


def pipelined(units, start, sample, slot_of, buffers, sems):
    for ahead in range(BUFFERS - 1):

        @pl.when(ahead < units)
        def _():
            start(ahead, buffers.at[ahead], sems.at[ahead])

    def body(unit, _):
        place = lax.rem(unit, BUFFERS)
        later = lax.rem(unit + BUFFERS - 1, BUFFERS)

        @pl.when(unit + BUFFERS - 1 < units)
        def _():
            start(unit + BUFFERS - 1, buffers.at[later], sems.at[later])

        pltpu.make_async_copy(sample, buffers.at[place], sems.at[place]).wait()
        split_store(buffers.at[place], slot_of(unit))
        return 0

    lax.fori_loop(0, units, body, 0)


def chip_body(ids, source, *refs, mine):
    packed, buffers, sems = refs[-3:]
    core = ids[1]
    first = 2 * core if mine else 2 * (1 - core)
    count = OWN + HALO

    def start(unit, buffer, sem):
        block = source.at[unit // count, lax.rem(unit, count) + core]
        pltpu.make_async_copy(block, buffer, sem).start()

    def slot_of(unit):
        return packed.at[first + unit // count, lax.rem(unit, count) + HALO * (1 - core)]

    pipelined(2 * count, start, source.at[0, 0], slot_of, buffers, sems)


def pick(number, values):
    result = jnp.int32(values[0])
    for index, value in enumerate(values[1:], 1):
        result = jnp.where(number == index, value, result)
    return result


def halo_body(ids, straight, cross, *refs, rows, slots, split):
    packed, buffers, sems = refs[-3:]
    row, core = ids[0], ids[1]
    units = len(slots[0])
    first = units // 2

    def start(unit, buffer, sem):
        by_straight = unit < first if split else core == 0
        place = lax.rem(unit, first) if split else unit

        @pl.when(by_straight)
        def _():
            pltpu.make_async_copy(straight.at[place], buffer, sem).start()

        @pl.when(jnp.logical_not(by_straight))
        def _():
            pltpu.make_async_copy(cross.at[place], buffer, sem).start()

    def slot_of(unit):
        number = unit + units * core
        return packed.at[
            pick(number, [layer for side in slots for layer, _ in side]),
            pick(number, [slot for side in slots for _, slot in side]),
        ]

    @pl.when((row >= rows[0]) & (row < rows[1]))
    def _():
        pipelined(units, start, straight.at[0], slot_of, buffers, sems)


PACKED = (GROUP, SLOTS, 3 * TILE, 4 * TILE)
PACK_SCRATCH = [
    pltpu.VMEM((BUFFERS, 3, 2, TILE, TILE), jnp.float32),
    pltpu.SemaphoreType.DMA((BUFFERS,)),
]


def pack_chip(ids, source, packed, mine):
    extra = () if packed is None else (packed,)
    return pl.pallas_call(
        functools.partial(chip_body, mine=mine),
        in_specs=[SMEM_SPEC, ANY_SPEC] + [VMEM_SPEC] * len(extra),
        out_specs=VMEM_SPEC,
        out_shape=jax.ShapeDtypeStruct(PACKED, jnp.bfloat16),
        scratch_shapes=PACK_SCRATCH,
        input_output_aliases={2: 0} if extra else {},
        compiler_params=PARAMS,
        cost_estimate=BRIEF,
        name="pack_mine" if mine else "pack_partner",
    )(ids, pltpu.with_memory_space_constraint(source, pltpu.HBM) if mine else source, *extra)


def pack_halo(ids, sources, packed, rows, slots, name, split=True):
    return pl.pallas_call(
        functools.partial(halo_body, rows=rows, slots=slots, split=split),
        in_specs=[SMEM_SPEC, ANY_SPEC, ANY_SPEC, VMEM_SPEC],
        out_specs=VMEM_SPEC,
        out_shape=jax.ShapeDtypeStruct(PACKED, jnp.bfloat16),
        scratch_shapes=PACK_SCRATCH,
        input_output_aliases={3: 0},
        compiler_params=PARAMS,
        cost_estimate=BRIEF,
        name=name,
    )(ids, *sources, packed)


def cut_body(ids, mine, other, straight, cross, sems, *, parts):
    row = ids[0]
    for begin_row, end_row, runs in parts:
        for side in range(2):

            @pl.when((row >= begin_row) & (row < end_row) & (ids[1] == side))
            def _():
                copies = []
                for out, entries in zip((straight, cross), runs[side]):
                    place = 0
                    for layer, begin, end in entries:
                        source = mine if layer // 2 == side else other
                        target = out.at[place : place + end - begin]
                        copies.append(
                            pltpu.make_async_copy(
                                source.at[layer % 2, begin:end], target, sems.at[len(copies)]
                            )
                        )
                        place += end - begin
                for copy in copies:
                    copy.start()
                for copy in copies:
                    copy.wait()


def cut(ids, mine, other, parts, name):
    count = sum(end - begin for _, begin, end in parts[0][2][0][0])
    return pl.pallas_call(
        functools.partial(cut_body, parts=parts),
        in_specs=[SMEM_SPEC, ANY_SPEC, ANY_SPEC],
        out_specs=[ANY_SPEC] * 2,
        out_shape=[pltpu.VMEM((count, 3, 2, TILE, TILE), jnp.float32)] * 2,
        scratch_shapes=[pltpu.SemaphoreType.DMA((6,))],
        compiler_params=PARAMS,
        cost_estimate=BRIEF,
        name=name,
    )(ids, pltpu.with_memory_space_constraint(mine, pltpu.HBM), other)


ROWS = 20


def rows_body(ids, cells, layers, rhs, couple, rows):
    strip = rhs.shape[-1]
    shot = lax.broadcasted_iota(jnp.int32, (8, strip), 0)
    position = lax.broadcasted_iota(jnp.int32, (8, strip), 1) + ids[2] * strip
    target = jnp.full((8, strip), -1, jnp.int32)
    depth = jnp.full((8, strip), -1, jnp.int32)
    for index in range(8):
        target = jnp.where(shot == index, cells[index], target)
        depth = jnp.where(shot == index, layers[index], depth)
    here = target == position
    for layer in range(2):
        hit = here & (depth == ids[3] * 2 + layer)
        rows[layer, 0:8] = rhs[0, layer] + jnp.where(hit, 4.0, 0.0)
        rows[layer, 8:16] = rhs[1, layer]
        for way in range(2):
            for part in range(2):
                spot = 16 + 2 * way + part
                rows[layer, spot : spot + 1] = couple[way, part, layer : layer + 1]


def edge_body(ids, rows, other, edge):
    for side in range(2):

        @pl.when(ids[1] == side)
        def _():
            mine, partner = slice(2 * side, 2 * side + 2), slice(2 - 2 * side, 4 - 2 * side)
            where = slice(HALF, 2 * HALF) if side == 0 else slice(0, HALF)
            edge[mine] = rows[:, :, where]
            edge[partner] = other[:, :, where]


def window_body(ids, rows, other, beside, window):
    for side in range(2):

        @pl.when(ids[1] == side)
        def _():
            mine, partner = slice(2 * side, 2 * side + 2), slice(2 - 2 * side, 4 - 2 * side)
            chip = slice(HALF, WINDOW) if side == 0 else slice(0, 2 * HALF)
            rest = slice(0, HALF) if side == 0 else slice(2 * HALF, WINDOW)
            window[mine, :, chip] = rows[...]
            window[partner, :, chip] = other[...]
            window[:, :, rest] = beside[...]


def small_call(body, smem, arrays, shape, name):
    return pl.pallas_call(
        body,
        in_specs=[SMEM_SPEC] * len(smem) + [VMEM_SPEC] * len(arrays),
        out_specs=VMEM_SPEC,
        out_shape=jax.ShapeDtypeStruct(shape, jnp.float32),
        compiler_params=PARAMS,
        cost_estimate=BRIEF,
        name=name,
    )(*smem, *arrays)


def store_parts(parts_ref, where, value):
    high = value.astype(jnp.bfloat16)
    parts_ref[0:16, where] = high
    parts_ref[16:32, where] = (value - high.astype(jnp.float32)).astype(jnp.bfloat16)


def scaled(coef_real, coef_imag, value):
    real, imag = value[0:8], value[8:16]
    return jnp.concatenate(
        [coef_real * real - coef_imag * imag, coef_real * imag + coef_imag * real], axis=0
    )


def tile_product(parts_ref, packed, layer, spot):
    product = jnp.dot(
        parts_ref[:, spot * TILE : (spot + 3) * TILE],
        packed[layer, spot],
        preferred_element_type=jnp.float32,
    )
    rows = product[0:16] + product[16:32]
    both = rows[:, 0 : 2 * TILE] + rows[:, 2 * TILE : 4 * TILE]
    real, imag = both[0:8], both[8:16]
    return jnp.concatenate(
        [real[:, 0:TILE] - imag[:, TILE:], real[:, TILE:] + imag[:, 0:TILE]], axis=0
    )


def lanes(start, stop):
    return slice(start * TILE, stop * TILE)


def down_operand(parts, window, layer, where, value):
    forcing = window[layer, 0:16, where]
    coef_real, coef_imag = window[layer, 16:17, where], window[layer, 17:18, where]
    store_parts(parts.at[layer % 2], where, forcing + scaled(coef_real, coef_imag, value))


def up_operand(parts, window, layer, where, value):
    coef_real, coef_imag = window[layer, 18:19, where], window[layer, 19:20, where]
    store_parts(parts.at[layer % 2], where, scaled(coef_real, coef_imag, value))


def down_layers(window, packed, waves, parts, layers):
    for layer in layers:
        reach = layers[-1] - layer
        for spot in range(HALO - reach, HALO + OWN + reach):
            value = tile_product(parts.at[layer % 2], packed, layer, spot)
            waves[layer, :, lanes(spot, spot + 1)] = value
            if reach:
                down_operand(parts, window, layer + 1, lanes(spot + 1, spot + 2), value)


def down_body(ids, low, mid, high, window, packed, _, out, waves, parts, *, turn):
    @pl.when(ids[0] == turn)
    def _():
        for index, source in enumerate((low, mid, high)):
            down_operand(parts, window, 0, lanes(4 * index, 4 * index + 4), source[...])
        down_layers(window, packed, waves, parts, range(GROUP))
        out[...] = waves[GROUP - 1, :, lanes(HALO, HALO + OWN)]


def pair_body(ids, low, mid, high, window, packed, _, *refs, turn, first):
    outs, waves, parts = refs[:-2], refs[-2], refs[-1]

    @pl.when(ids[0] == turn)
    def _():
        if first:
            waves[1, :, lanes(1, 3)] = low[...]
            waves[1, :, lanes(7, 9)] = high[...]
            down_operand(parts, window, first, lanes(2, 10), waves[1, :, lanes(1, 9)])
        else:
            down_operand(parts, window, first, lanes(2, 4), low[:, lanes(2, 4)])
            down_operand(parts, window, first, lanes(4, 8), mid[...])
            down_operand(parts, window, first, lanes(8, 10), high[:, lanes(0, 2)])
        down_layers(window, packed, waves, parts, (first, first + 1))
        if first:
            outs[0][...] = waves[3, :, lanes(HALO, HALO + OWN)]
        else:
            outs[0][...] = waves[1, :, lanes(HALO, HALO + 2)]
            outs[1][...] = waves[1, :, lanes(HALO + 2, HALO + OWN)]


def up_body(ids, low, mid, high, window, packed, waves, left, right, _, out, field, parts, *, turn):
    @pl.when(ids[0] == turn)
    def _():
        for index, source in enumerate((low, mid, high)):
            up_operand(parts, window, GROUP - 1, lanes(4 * index, 4 * index + 4), source[...])
        for layer in reversed(range(GROUP)):
            for spot in range(HALO - layer, HALO + OWN + layer):
                if layer >= 2 and spot < HALO:
                    wave = left[layer - 2, :, lanes(spot + 1, spot + 2)]
                elif layer >= 2 and spot >= HALO + OWN:
                    wave = right[layer - 2, :, lanes(spot - HALO - OWN, spot - HALO - OWN + 1)]
                else:
                    wave = waves[layer, :, lanes(spot, spot + 1)]
                value = wave + tile_product(parts.at[layer % 2], packed, layer, spot)
                if layer:
                    up_operand(parts, window, layer - 1, lanes(spot + 1, spot + 2), value)
                if HALO <= spot < HALO + OWN:
                    field[layer, :, lanes(spot - HALO, spot - HALO + 1)] = value
        out[...] = field[0]


PARTS = pltpu.VMEM((2, 32, WINDOW), jnp.bfloat16)


def down_step(ids, received, window, packed, waves, turn):
    return pl.pallas_call(
        functools.partial(down_body, turn=turn),
        in_specs=[SMEM_SPEC] + [VMEM_SPEC] * 6,
        out_specs=(VMEM_SPEC, VMEM_SPEC),
        out_shape=(
            jax.ShapeDtypeStruct((16, HALF), jnp.float32),
            jax.ShapeDtypeStruct((GROUP, 16, SPAN), jnp.float32),
        ),
        scratch_shapes=[PARTS],
        input_output_aliases={6: 1},
        compiler_params=PARAMS,
        cost_estimate=BRIEF,
        name=f"down_{turn}",
    )(ids, *received, window, packed, waves)


def pair_step(ids, low, mid, high, window, packed, waves, turn, first):
    widths = (HALF,) if first else (2 * TILE, 2 * TILE)
    return pl.pallas_call(
        functools.partial(pair_body, turn=turn, first=first),
        in_specs=[SMEM_SPEC] + [VMEM_SPEC] * 6,
        out_specs=(VMEM_SPEC,) * (len(widths) + 1),
        out_shape=tuple(jax.ShapeDtypeStruct((16, width), jnp.float32) for width in widths)
        + (jax.ShapeDtypeStruct((GROUP, 16, SPAN), jnp.float32),),
        scratch_shapes=[PARTS],
        input_output_aliases={6: len(widths)},
        compiler_params=PARAMS,
        cost_estimate=BRIEF,
        name=f"pair_{turn}_{first}",
    )(ids, low, mid, high, window, packed, waves)


def up_step(ids, received, window, packed, waves, left, right, field, turn):
    return pl.pallas_call(
        functools.partial(up_body, turn=turn),
        in_specs=[SMEM_SPEC] + [VMEM_SPEC] * 9,
        out_specs=(VMEM_SPEC, VMEM_SPEC),
        out_shape=(
            jax.ShapeDtypeStruct((16, HALF), jnp.float32),
            jax.ShapeDtypeStruct((GROUP, 16, HALF), jnp.float32),
        ),
        scratch_shapes=[PARTS],
        input_output_aliases={9: 1},
        compiler_params=PARAMS,
        cost_estimate=BRIEF,
        name=f"up_{turn}",
    )(ids, *received, window, packed, waves, left, right, field)


def give_body(ids, waves, field, give):
    own = slice(HALO * TILE, (HALO + OWN) * TILE)
    for side in range(2):

        @pl.when(ids[1] == side)
        def _():
            partner = slice(2 - 2 * side, 4 - 2 * side)
            give[0] = waves[partner, :, own]
            give[1] = field[partner]


def join_body(ids, waves, field, taken, out_waves, out_field):
    for side in range(2):

        @pl.when(ids[1] == side)
        def _():
            mine = slice(HALF * side, HALF * (side + 1))
            partner = slice(HALF * (1 - side), HALF * (2 - side))
            for layer in range(2):
                for part in range(2):
                    rows = slice(8 * part, 8 * (part + 1))
                    own = slice(HALO * TILE, (HALO + OWN) * TILE)
                    out_waves[part, layer, :, mine] = waves[2 * side + layer, rows, own]
                    out_field[part, layer, :, mine] = field[2 * side + layer, rows]
                    out_waves[part, layer, :, partner] = taken[0, layer, rows]
                    out_field[part, layer, :, partner] = taken[1, layer, rows]


def join(ids, waves, field, taken, shape):
    return pl.pallas_call(
        join_body,
        in_specs=[SMEM_SPEC] + [VMEM_SPEC] * 3,
        out_specs=(VMEM_SPEC,) * 2,
        out_shape=(jax.ShapeDtypeStruct(shape, jnp.float32),) * 2,
        compiler_params=PARAMS,
        cost_estimate=BRIEF,
        name="join",
    )(ids, waves, field, taken)


PAIR_ROWS = 2
LATE_ROWS = 5
FIRST_RUNS = (
    (((0, 7, 8),), ((0, 0, 1),)),
    (((2, 0, 1),), ((2, 7, 8),)),
)
FIRST_SLOTS = (((0, 2), (2, 2)), ((2, 7), (0, 7)))
DOWN_RUNS = (
    (((0, 5, 7), (1, 6, 8)), ((0, 1, 3), (1, 0, 2))),
    ((), ()),
)
DOWN_SLOTS = (
    ((0, 0), (0, 1), (1, 1), (1, 2)),
    ((0, 8), (0, 9), (1, 7), (1, 8)),
)
EARLY_RUNS = (
    (((3, 7, 8), (2, 6, 7)), ((3, 0, 1), (2, 1, 2))),
    (((3, 1, 3),), ((3, 5, 7),)),
)
EARLY_SLOTS = (
    ((3, 2), (2, 1), (3, 0), (3, 1)),
    ((3, 8), (3, 9), (3, 7), (2, 8)),
)
LAST_RUNS = ((((1, 7, 8),), ((1, 0, 1),)), ((), ()))
LAST_SLOTS = (((1, 2),), ((1, 7),))


def gated(value, *others):
    return lax.optimization_barrier((value, *others))[0]


def shards(rhs_field, src_cell, src_layer, factor, couple):
    layer_total, shot_count, strip_cells = rhs_field.shape[1:]
    depth_count, lat_count = lax.axis_size("depth"), lax.axis_size("lat")
    depth_pos, lat_pos = lax.axis_index("depth"), lax.axis_index("lat")
    core = lax.rem(depth_pos, 2)
    first_core = core == 0
    chip_rows = depth_count // 2
    halves = 2 * lat_count
    everyone = range(chip_rows)
    ids = jnp.stack([depth_pos // 2, core, lat_pos, depth_pos]).astype(jnp.int32)

    def device(row, half):
        return (2 * row + half % 2) * lat_count + half // 2

    def at(depth, lat):
        return depth * lat_count + lat

    def hop(value, rows, step, shift):
        pairs = [
            (device(row, half), device(row + step, half + shift))
            for row in rows
            if 0 <= row + step < chip_rows
            for half in range(halves)
            if 0 <= half + shift < halves
        ]
        return lax.ppermute(value, AXES, pairs)

    partner = [(at(d, l), at(d ^ 1, l)) for d in range(depth_count) for l in range(lat_count)]

    def beside_pairs(rows, same, sides=(0, 1)):
        pairs = []
        for row in rows:
            for side in sides:
                shift = 1 if (side == 0) == same else -1
                target = side if same else 1 - side
                pairs += [
                    (at(2 * row + side, l), at(2 * row + target, l + shift))
                    for l in range(lat_count)
                    if 0 <= l + shift < lat_count
                ]
        return pairs

    def send_halo(ids, other, parts, name, sides=(0, 1), after=()):
        straight, cross = cut(ids, factor, other, parts, name)
        straight, cross = lax.optimization_barrier((straight, cross, *after))[:2]
        rows = [row for begin, end, _ in parts for row in range(begin, end)]
        return straight, (
            lax.ppermute(straight, AXES, beside_pairs(rows, True, sides)),
            lax.ppermute(cross, AXES, beside_pairs(rows, False, sides)),
        )

    first_cut, first_halo = send_halo(ids, factor, ((0, chip_rows, FIRST_RUNS),), "cut_first")
    down_parts = ((PAIR_ROWS, chip_rows, DOWN_RUNS),)
    early_parts = ((LATE_ROWS, chip_rows, EARLY_RUNS),)
    late_parts = ((0, LATE_ROWS, EARLY_RUNS),)
    last_parts = ((0, PAIR_ROWS, LAST_RUNS),)
    other = lax.ppermute(gated(factor, first_cut), AXES, partner)

    rows = small_call(
        rows_body,
        (gated(ids, first_cut), src_cell, src_layer),
        (rhs_field, couple),
        (layer_total, ROWS, strip_cells),
        "rows",
    )
    rows_other = lax.ppermute(rows, AXES, partner)
    packed = pack_chip(gated(ids, rows), factor, None, True)
    edge = small_call(
        edge_body, (gated(ids, packed),), (rows, rows_other), (GROUP, ROWS, HALF), "edge"
    )
    packed = pack_chip(ids, other, packed, False)
    beside = lax.ppermute(edge, AXES, beside_pairs(everyone, True))
    window = small_call(
        window_body, (gated(ids, packed, *first_halo),), (rows, rows_other, beside), (GROUP, ROWS, WINDOW), "window"
    )
    _, halo = send_halo(gated(ids, rows), factor, down_parts, "cut_down", (0,), (window, *first_halo))
    packed = pack_halo(
        gated(ids, window), first_halo, packed, (0, chip_rows), FIRST_SLOTS, "halo_first"
    )

    zero_half = jnp.zeros((2 * shot_count, HALF), jnp.float32)
    waves = jnp.zeros((GROUP, 2 * shot_count, SPAN), jnp.float32)
    field = jnp.zeros((GROUP, 2 * shot_count, HALF), jnp.float32)

    received = (zero_half,) * 3
    for turn in everyone:
        if turn < PAIR_ROWS:
            left_edge, right_edge, waves = pair_step(
                ids, *received, window, packed, waves, turn, 0
            )
            pairs = range(PAIR_ROWS)
            low, high = hop(right_edge, pairs, 0, 1), hop(left_edge, pairs, 0, -1)
            out, waves = pair_step(ids, low, left_edge, high, window, packed, waves, turn, 2)
            if turn + 1 == PAIR_ROWS:
                down_rows = (PAIR_ROWS, chip_rows)
                packed = pack_halo(
                    gated(ids, out), halo, packed, down_rows, DOWN_SLOTS, "halo_down", False
                )
                _, early_halo = send_halo(gated(ids, out, *halo), other, early_parts, "cut_early")
                out, packed = lax.optimization_barrier((out, packed))
        else:
            out, waves = down_step(ids, received, window, packed, waves, turn)
            if turn == LATE_ROWS:
                late_ids, last_rows = gated(ids, out), (LATE_ROWS + 1, chip_rows)
                packed = pack_halo(late_ids, early_halo, packed, last_rows, EARLY_SLOTS, "halo_last")
                out, packed = lax.optimization_barrier((out, packed))
                _, late_halo = send_halo(gated(ids, out), other, late_parts, "cut_late")
        if turn + 1 < chip_rows:
            group = range(turn % 3, chip_rows, 3)
            received = (hop(out, group, 1, 1), hop(out, group, 1, 0), hop(out, group, 1, -1))

    deep = waves[2:, :, HALO * TILE : (HALO + OWN) * TILE]
    left, right = hop(deep, everyone, 0, 1), hop(deep, everyone, 0, -1)
    received = (zero_half,) * 3
    for turn in reversed(everyone):
        out, field = up_step(ids, received, window, packed, waves, left, right, field, turn)
        if turn == LATE_ROWS + 1:
            row = (LATE_ROWS, LATE_ROWS + 1)
            packed = pack_halo(gated(ids, out), early_halo, packed, row, EARLY_SLOTS, "halo_early")
            out, packed = lax.optimization_barrier((out, packed))
        if turn == LATE_ROWS:
            late_rows = (0, LATE_ROWS)
            packed = pack_halo(gated(ids, out), late_halo, packed, late_rows, EARLY_SLOTS, "halo_late")
            out, packed = lax.optimization_barrier((out, packed))
        if turn == LATE_ROWS - 1:
            _, last_halo = send_halo(gated(ids, out), factor, last_parts, "cut_last", (0,))
        if turn == PAIR_ROWS:
            last_rows = (0, PAIR_ROWS)
            packed = pack_halo(
                gated(ids, out), last_halo, packed, last_rows, LAST_SLOTS, "halo_extra", False
            )
            out, packed = lax.optimization_barrier((out, packed))
        if turn:
            group = range(turn % 3, chip_rows, 3)
            received = (hop(out, group, -1, 1), hop(out, group, -1, 0), hop(out, group, -1, -1))

    shape = (2, layer_total, 2 * shot_count, HALF)
    waves = gated(waves, field)
    give = small_call(give_body, (ids,), (waves, field), shape, "give")
    taken = lax.ppermute(give, AXES, partner)
    return join(ids, waves, field, taken, rhs_field.shape)


def solution(mesh):
    placed = (
        P(None, "depth", None, "lat"),
        P(),
        P(),
        P("depth", "lat", None, None, None, None),
        P(None, None, "depth", "lat"),
    )
    return jax.shard_map(
        shards,
        mesh=mesh,
        in_specs=placed,
        out_specs=(P(None, "depth", None, "lat"), P(None, "depth", None, "lat")),
        check_vma=False,
    )
```

```python
import functools

import jax
import jax.numpy as jnp
from jax import lax
from jax.experimental import pallas as pl
from jax.experimental.pallas import tpu as pltpu
from jax.sharding import PartitionSpec as P

TILE = 128
GROUP = 4
OWN = 4
HALO = 3
SLOTS = OWN + 2 * HALO
WINDOW = (OWN + 2 * (HALO + 1)) * TILE
SPAN = SLOTS * TILE
HALF = OWN * TILE
VMEM_LIMIT = 10 << 20

VMEM_SPEC = pl.BlockSpec(memory_space=pltpu.VMEM)
SMEM_SPEC = pl.BlockSpec(memory_space=pltpu.SMEM)
ANY_SPEC = pl.BlockSpec(memory_space=pl.ANY)
PARAMS = pltpu.CompilerParams(vmem_limit_bytes=VMEM_LIMIT)
BRIEF = pl.CostEstimate(flops=1, transcendentals=0, bytes_accessed=1)
AXES = ("depth", "lat")


def split_store(buffer, slot_ref):
    for offset in range(3):
        for part in range(2):
            block = buffer[offset, part]
            high = block.astype(jnp.bfloat16)
            low = (block - high.astype(jnp.float32)).astype(jnp.bfloat16)
            rows = slice(offset * TILE, (offset + 1) * TILE)
            slot_ref[rows, part * TILE : (part + 1) * TILE] = high
            slot_ref[rows, (2 + part) * TILE : (3 + part) * TILE] = low


BUFFERS = 4


def pipelined(units, start, sample, slot_of, buffers, sems):
    for ahead in range(BUFFERS - 1):

        @pl.when(ahead < units)
        def _():
            start(ahead, buffers.at[ahead], sems.at[ahead])

    def body(unit, _):
        place = lax.rem(unit, BUFFERS)
        later = lax.rem(unit + BUFFERS - 1, BUFFERS)

        @pl.when(unit + BUFFERS - 1 < units)
        def _():
            start(unit + BUFFERS - 1, buffers.at[later], sems.at[later])

        pltpu.make_async_copy(sample, buffers.at[place], sems.at[place]).wait()
        split_store(buffers.at[place], slot_of(unit))
        return 0

    lax.fori_loop(0, units, body, 0)


def chip_body(ids, source, *refs, mine):
    packed, buffers, sems = refs[-3:]
    core = ids[1]
    first = 2 * core if mine else 2 * (1 - core)
    count = OWN + HALO

    def start(unit, buffer, sem):
        block = source.at[unit // count, lax.rem(unit, count) + core]
        pltpu.make_async_copy(block, buffer, sem).start()

    def slot_of(unit):
        return packed.at[first + unit // count, lax.rem(unit, count) + HALO * (1 - core)]

    pipelined(2 * count, start, source.at[0, 0], slot_of, buffers, sems)


def pick(number, values):
    result = jnp.int32(values[0])
    for index, value in enumerate(values[1:], 1):
        result = jnp.where(number == index, value, result)
    return result


def halo_body(ids, straight, cross, *refs, rows, slots, split):
    packed, buffers, sems = refs[-3:]
    row, core = ids[0], ids[1]
    units = len(slots[0])
    first = units // 2

    def start(unit, buffer, sem):
        by_straight = unit < first if split else core == 0
        place = lax.rem(unit, first) if split else unit

        @pl.when(by_straight)
        def _():
            pltpu.make_async_copy(straight.at[place], buffer, sem).start()

        @pl.when(jnp.logical_not(by_straight))
        def _():
            pltpu.make_async_copy(cross.at[place], buffer, sem).start()

    def slot_of(unit):
        number = unit + units * core
        return packed.at[
            pick(number, [layer for side in slots for layer, _ in side]),
            pick(number, [slot for side in slots for _, slot in side]),
        ]

    @pl.when((row >= rows[0]) & (row < rows[1]))
    def _():
        pipelined(units, start, straight.at[0], slot_of, buffers, sems)


PACKED = (GROUP, SLOTS, 3 * TILE, 4 * TILE)
PACK_SCRATCH = [
    pltpu.VMEM((BUFFERS, 3, 2, TILE, TILE), jnp.float32),
    pltpu.SemaphoreType.DMA((BUFFERS,)),
]


def pack_chip(ids, source, packed, mine):
    extra = () if packed is None else (packed,)
    return pl.pallas_call(
        functools.partial(chip_body, mine=mine),
        in_specs=[SMEM_SPEC, ANY_SPEC] + [VMEM_SPEC] * len(extra),
        out_specs=VMEM_SPEC,
        out_shape=jax.ShapeDtypeStruct(PACKED, jnp.bfloat16),
        scratch_shapes=PACK_SCRATCH,
        input_output_aliases={2: 0} if extra else {},
        compiler_params=PARAMS,
        cost_estimate=BRIEF,
        name="pack_mine" if mine else "pack_partner",
    )(ids, pltpu.with_memory_space_constraint(source, pltpu.HBM) if mine else source, *extra)


def pack_halo(ids, sources, packed, rows, slots, name, split=True):
    return pl.pallas_call(
        functools.partial(halo_body, rows=rows, slots=slots, split=split),
        in_specs=[SMEM_SPEC, ANY_SPEC, ANY_SPEC, VMEM_SPEC],
        out_specs=VMEM_SPEC,
        out_shape=jax.ShapeDtypeStruct(PACKED, jnp.bfloat16),
        scratch_shapes=PACK_SCRATCH,
        input_output_aliases={3: 0},
        compiler_params=PARAMS,
        cost_estimate=BRIEF,
        name=name,
    )(ids, *sources, packed)


def cut_body(ids, mine, other, straight, cross, sems, *, parts):
    row = ids[0]
    for begin_row, end_row, runs in parts:
        for side in range(2):

            @pl.when((row >= begin_row) & (row < end_row) & (ids[1] == side))
            def _():
                copies = []
                for out, entries in zip((straight, cross), runs[side]):
                    place = 0
                    for layer, begin, end in entries:
                        source = mine if layer // 2 == side else other
                        target = out.at[place : place + end - begin]
                        copies.append(
                            pltpu.make_async_copy(
                                source.at[layer % 2, begin:end], target, sems.at[len(copies)]
                            )
                        )
                        place += end - begin
                for copy in copies:
                    copy.start()
                for copy in copies:
                    copy.wait()


def cut(ids, mine, other, parts, name):
    count = sum(end - begin for _, begin, end in parts[0][2][0][0])
    return pl.pallas_call(
        functools.partial(cut_body, parts=parts),
        in_specs=[SMEM_SPEC, ANY_SPEC, ANY_SPEC],
        out_specs=[ANY_SPEC] * 2,
        out_shape=[pltpu.VMEM((count, 3, 2, TILE, TILE), jnp.float32)] * 2,
        scratch_shapes=[pltpu.SemaphoreType.DMA((6,))],
        compiler_params=PARAMS,
        cost_estimate=BRIEF,
        name=name,
    )(ids, pltpu.with_memory_space_constraint(mine, pltpu.HBM), other)


ROWS = 20


def rows_body(ids, cells, layers, rhs, couple, rows):
    strip = rhs.shape[-1]
    shot = lax.broadcasted_iota(jnp.int32, (8, strip), 0)
    position = lax.broadcasted_iota(jnp.int32, (8, strip), 1) + ids[2] * strip
    target = jnp.full((8, strip), -1, jnp.int32)
    depth = jnp.full((8, strip), -1, jnp.int32)
    for index in range(8):
        target = jnp.where(shot == index, cells[index], target)
        depth = jnp.where(shot == index, layers[index], depth)
    here = target == position
    for layer in range(2):
        hit = here & (depth == ids[3] * 2 + layer)
        rows[layer, 0:8] = rhs[0, layer] + jnp.where(hit, 4.0, 0.0)
        rows[layer, 8:16] = rhs[1, layer]
        for way in range(2):
            for part in range(2):
                spot = 16 + 2 * way + part
                rows[layer, spot : spot + 1] = couple[way, part, layer : layer + 1]


def edge_body(ids, rows, other, edge):
    for side in range(2):

        @pl.when(ids[1] == side)
        def _():
            mine, partner = slice(2 * side, 2 * side + 2), slice(2 - 2 * side, 4 - 2 * side)
            where = slice(HALF, 2 * HALF) if side == 0 else slice(0, HALF)
            edge[mine] = rows[:, :, where]
            edge[partner] = other[:, :, where]


def window_body(ids, rows, other, beside, window):
    for side in range(2):

        @pl.when(ids[1] == side)
        def _():
            mine, partner = slice(2 * side, 2 * side + 2), slice(2 - 2 * side, 4 - 2 * side)
            chip = slice(HALF, WINDOW) if side == 0 else slice(0, 2 * HALF)
            rest = slice(0, HALF) if side == 0 else slice(2 * HALF, WINDOW)
            window[mine, :, chip] = rows[...]
            window[partner, :, chip] = other[...]
            window[:, :, rest] = beside[...]


def small_call(body, smem, arrays, shape, name):
    return pl.pallas_call(
        body,
        in_specs=[SMEM_SPEC] * len(smem) + [VMEM_SPEC] * len(arrays),
        out_specs=VMEM_SPEC,
        out_shape=jax.ShapeDtypeStruct(shape, jnp.float32),
        compiler_params=PARAMS,
        cost_estimate=BRIEF,
        name=name,
    )(*smem, *arrays)


def store_parts(parts_ref, where, value):
    high = value.astype(jnp.bfloat16)
    parts_ref[0:16, where] = high
    parts_ref[16:32, where] = (value - high.astype(jnp.float32)).astype(jnp.bfloat16)


def scaled(coef_real, coef_imag, value):
    real, imag = value[0:8], value[8:16]
    return jnp.concatenate(
        [coef_real * real - coef_imag * imag, coef_real * imag + coef_imag * real], axis=0
    )


def tile_product(parts_ref, packed, layer, spot):
    product = jnp.dot(
        parts_ref[:, spot * TILE : (spot + 3) * TILE],
        packed[layer, spot],
        preferred_element_type=jnp.float32,
    )
    rows = product[0:16] + product[16:32]
    both = rows[:, 0 : 2 * TILE] + rows[:, 2 * TILE : 4 * TILE]
    real, imag = both[0:8], both[8:16]
    return jnp.concatenate(
        [real[:, 0:TILE] - imag[:, TILE:], real[:, TILE:] + imag[:, 0:TILE]], axis=0
    )


def lanes(start, stop):
    return slice(start * TILE, stop * TILE)


def down_operand(parts, window, layer, where, value):
    forcing = window[layer, 0:16, where]
    coef_real, coef_imag = window[layer, 16:17, where], window[layer, 17:18, where]
    store_parts(parts.at[layer % 2], where, forcing + scaled(coef_real, coef_imag, value))


def up_operand(parts, window, layer, where, value):
    coef_real, coef_imag = window[layer, 18:19, where], window[layer, 19:20, where]
    store_parts(parts.at[layer % 2], where, scaled(coef_real, coef_imag, value))


def down_layers(window, packed, waves, parts, layers):
    for layer in layers:
        reach = layers[-1] - layer
        for spot in range(HALO - reach, HALO + OWN + reach):
            value = tile_product(parts.at[layer % 2], packed, layer, spot)
            waves[layer, :, lanes(spot, spot + 1)] = value
            if reach:
                down_operand(parts, window, layer + 1, lanes(spot + 1, spot + 2), value)


def my_turn(turn):
    return lax.axis_index("depth") // 2 == turn


def down_body(low, mid, high, window, packed, _, out, waves, parts, *, turn):
    @pl.when(my_turn(turn))
    def _():
        for index, source in enumerate((low, mid, high)):
            down_operand(parts, window, 0, lanes(4 * index, 4 * index + 4), source[...])
        down_layers(window, packed, waves, parts, range(GROUP))
        out[...] = waves[GROUP - 1, :, lanes(HALO, HALO + OWN)]


def pair_body(low, mid, high, window, packed, _, *refs, turn, first):
    outs, waves, parts = refs[:-2], refs[-2], refs[-1]

    @pl.when(my_turn(turn))
    def _():
        if first:
            waves[1, :, lanes(1, 3)] = low[...]
            waves[1, :, lanes(7, 9)] = high[...]
            down_operand(parts, window, first, lanes(2, 10), waves[1, :, lanes(1, 9)])
        else:
            down_operand(parts, window, first, lanes(2, 4), low[:, lanes(2, 4)])
            down_operand(parts, window, first, lanes(4, 8), mid[...])
            down_operand(parts, window, first, lanes(8, 10), high[:, lanes(0, 2)])
        down_layers(window, packed, waves, parts, (first, first + 1))
        if first:
            outs[0][...] = waves[3, :, lanes(HALO, HALO + OWN)]
        else:
            outs[0][...] = waves[1, :, lanes(HALO, HALO + 2)]
            outs[1][...] = waves[1, :, lanes(HALO + 2, HALO + OWN)]


def up_body(low, mid, high, window, packed, waves, left, right, _, out, field, parts, *, turn):
    @pl.when(my_turn(turn))
    def _():
        for index, source in enumerate((low, mid, high)):
            up_operand(parts, window, GROUP - 1, lanes(4 * index, 4 * index + 4), source[...])
        for layer in reversed(range(GROUP)):
            for spot in range(HALO - layer, HALO + OWN + layer):
                if layer >= 2 and spot < HALO:
                    wave = left[layer - 2, :, lanes(spot + 1, spot + 2)]
                elif layer >= 2 and spot >= HALO + OWN:
                    wave = right[layer - 2, :, lanes(spot - HALO - OWN, spot - HALO - OWN + 1)]
                else:
                    wave = waves[layer, :, lanes(spot, spot + 1)]
                value = wave + tile_product(parts.at[layer % 2], packed, layer, spot)
                if layer:
                    up_operand(parts, window, layer - 1, lanes(spot + 1, spot + 2), value)
                if HALO <= spot < HALO + OWN:
                    field[layer, :, lanes(spot - HALO, spot - HALO + 1)] = value
        out[...] = field[0]


PARTS = pltpu.VMEM((2, 32, WINDOW), jnp.bfloat16)


def down_step(received, window, packed, waves, turn):
    return pl.pallas_call(
        functools.partial(down_body, turn=turn),
        in_specs=[VMEM_SPEC] * 6,
        out_specs=(VMEM_SPEC, VMEM_SPEC),
        out_shape=(
            jax.ShapeDtypeStruct((16, HALF), jnp.float32),
            jax.ShapeDtypeStruct((GROUP, 16, SPAN), jnp.float32),
        ),
        scratch_shapes=[PARTS],
        input_output_aliases={5: 1},
        compiler_params=PARAMS,
        cost_estimate=BRIEF,
        name=f"down_{turn}",
    )(*received, window, packed, waves)


def pair_step(low, mid, high, window, packed, waves, turn, first):
    widths = (HALF,) if first else (2 * TILE, 2 * TILE)
    return pl.pallas_call(
        functools.partial(pair_body, turn=turn, first=first),
        in_specs=[VMEM_SPEC] * 6,
        out_specs=(VMEM_SPEC,) * (len(widths) + 1),
        out_shape=tuple(jax.ShapeDtypeStruct((16, width), jnp.float32) for width in widths)
        + (jax.ShapeDtypeStruct((GROUP, 16, SPAN), jnp.float32),),
        scratch_shapes=[PARTS],
        input_output_aliases={5: len(widths)},
        compiler_params=PARAMS,
        cost_estimate=BRIEF,
        name=f"pair_{turn}_{first}",
    )(low, mid, high, window, packed, waves)


def up_step(received, window, packed, waves, left, right, field, turn):
    return pl.pallas_call(
        functools.partial(up_body, turn=turn),
        in_specs=[VMEM_SPEC] * 9,
        out_specs=(VMEM_SPEC, VMEM_SPEC),
        out_shape=(
            jax.ShapeDtypeStruct((16, HALF), jnp.float32),
            jax.ShapeDtypeStruct((GROUP, 16, HALF), jnp.float32),
        ),
        scratch_shapes=[PARTS],
        input_output_aliases={8: 1},
        compiler_params=PARAMS,
        cost_estimate=BRIEF,
        name=f"up_{turn}",
    )(*received, window, packed, waves, left, right, field)


def give_body(ids, waves, field, give):
    own = slice(HALO * TILE, (HALO + OWN) * TILE)
    for side in range(2):

        @pl.when(ids[1] == side)
        def _():
            partner = slice(2 - 2 * side, 4 - 2 * side)
            give[0] = waves[partner, :, own]
            give[1] = field[partner]


def join_body(ids, waves, field, taken, out_waves, out_field):
    for side in range(2):

        @pl.when(ids[1] == side)
        def _():
            mine = slice(HALF * side, HALF * (side + 1))
            partner = slice(HALF * (1 - side), HALF * (2 - side))
            for layer in range(2):
                for part in range(2):
                    rows = slice(8 * part, 8 * (part + 1))
                    own = slice(HALO * TILE, (HALO + OWN) * TILE)
                    out_waves[part, layer, :, mine] = waves[2 * side + layer, rows, own]
                    out_field[part, layer, :, mine] = field[2 * side + layer, rows]
                    out_waves[part, layer, :, partner] = taken[0, layer, rows]
                    out_field[part, layer, :, partner] = taken[1, layer, rows]


def join(ids, waves, field, taken, shape):
    return pl.pallas_call(
        join_body,
        in_specs=[SMEM_SPEC] + [VMEM_SPEC] * 3,
        out_specs=(VMEM_SPEC,) * 2,
        out_shape=(jax.ShapeDtypeStruct(shape, jnp.float32),) * 2,
        compiler_params=PARAMS,
        cost_estimate=BRIEF,
        name="join",
    )(ids, waves, field, taken)


PAIR_ROWS = 2
LATE_ROWS = 5
FIRST_RUNS = (
    (((0, 7, 8),), ((0, 0, 1),)),
    (((2, 0, 1),), ((2, 7, 8),)),
)
FIRST_SLOTS = (((0, 2), (2, 2)), ((2, 7), (0, 7)))
DOWN_RUNS = (
    (((0, 5, 7), (1, 6, 8)), ((0, 1, 3), (1, 0, 2))),
    ((), ()),
)
DOWN_SLOTS = (
    ((0, 0), (0, 1), (1, 1), (1, 2)),
    ((0, 8), (0, 9), (1, 7), (1, 8)),
)
EARLY_RUNS = (
    (((3, 7, 8), (2, 6, 7)), ((3, 0, 1), (2, 1, 2))),
    (((3, 1, 3),), ((3, 5, 7),)),
)
EARLY_SLOTS = (
    ((3, 2), (2, 1), (3, 0), (3, 1)),
    ((3, 8), (3, 9), (3, 7), (2, 8)),
)
LAST_RUNS = ((((1, 7, 8),), ((1, 0, 1),)), ((), ()))
LAST_SLOTS = (((1, 2),), ((1, 7),))


def gated(value, *others):
    return lax.optimization_barrier((value, *others))[0]


def shards(rhs_field, src_cell, src_layer, factor, couple):
    layer_total, shot_count, strip_cells = rhs_field.shape[1:]
    depth_count, lat_count = lax.axis_size("depth"), lax.axis_size("lat")
    depth_pos, lat_pos = lax.axis_index("depth"), lax.axis_index("lat")
    core = lax.rem(depth_pos, 2)
    first_core = core == 0
    chip_rows = depth_count // 2
    halves = 2 * lat_count
    everyone = range(chip_rows)
    ids = jnp.stack([depth_pos // 2, core, lat_pos, depth_pos]).astype(jnp.int32)

    def device(row, half):
        return (2 * row + half % 2) * lat_count + half // 2

    def at(depth, lat):
        return depth * lat_count + lat

    def hop(value, rows, step, shift):
        pairs = [
            (device(row, half), device(row + step, half + shift))
            for row in rows
            if 0 <= row + step < chip_rows
            for half in range(halves)
            if 0 <= half + shift < halves
        ]
        return lax.ppermute(value, AXES, pairs)

    partner = [(at(d, l), at(d ^ 1, l)) for d in range(depth_count) for l in range(lat_count)]

    def beside_pairs(rows, same, sides=(0, 1)):
        pairs = []
        for row in rows:
            for side in sides:
                shift = 1 if (side == 0) == same else -1
                target = side if same else 1 - side
                pairs += [
                    (at(2 * row + side, l), at(2 * row + target, l + shift))
                    for l in range(lat_count)
                    if 0 <= l + shift < lat_count
                ]
        return pairs

    def send_halo(ids, other, parts, name, sides=(0, 1), after=()):
        straight, cross = cut(ids, factor, other, parts, name)
        straight, cross = lax.optimization_barrier((straight, cross, *after))[:2]
        rows = [row for begin, end, _ in parts for row in range(begin, end)]
        return straight, (
            lax.ppermute(straight, AXES, beside_pairs(rows, True, sides)),
            lax.ppermute(cross, AXES, beside_pairs(rows, False, sides)),
        )

    first_cut, first_halo = send_halo(ids, factor, ((0, chip_rows, FIRST_RUNS),), "cut_first")
    down_parts = ((PAIR_ROWS, chip_rows, DOWN_RUNS),)
    early_parts = ((LATE_ROWS, chip_rows, EARLY_RUNS),)
    late_parts = ((0, LATE_ROWS, EARLY_RUNS),)
    last_parts = ((0, PAIR_ROWS, LAST_RUNS),)
    other = lax.ppermute(gated(factor, first_cut), AXES, partner)

    rows = small_call(
        rows_body,
        (gated(ids, first_cut), src_cell, src_layer),
        (rhs_field, couple),
        (layer_total, ROWS, strip_cells),
        "rows",
    )
    rows_other = lax.ppermute(rows, AXES, partner)
    packed = pack_chip(gated(ids, rows), factor, None, True)
    edge = small_call(
        edge_body, (gated(ids, packed),), (rows, rows_other), (GROUP, ROWS, HALF), "edge"
    )
    packed = pack_chip(ids, other, packed, False)
    beside = lax.ppermute(edge, AXES, beside_pairs(everyone, True))
    window = small_call(
        window_body, (gated(ids, packed, *first_halo),), (rows, rows_other, beside), (GROUP, ROWS, WINDOW), "window"
    )
    _, halo = send_halo(gated(ids, rows), factor, down_parts, "cut_down", (0,), (window, *first_halo))
    packed = pack_halo(
        gated(ids, window), first_halo, packed, (0, chip_rows), FIRST_SLOTS, "halo_first"
    )

    zero_half = jnp.zeros((2 * shot_count, HALF), jnp.float32)
    waves = jnp.zeros((GROUP, 2 * shot_count, SPAN), jnp.float32)
    field = jnp.zeros((GROUP, 2 * shot_count, HALF), jnp.float32)

    received = (zero_half,) * 3
    for turn in everyone:
        if turn < PAIR_ROWS:
            left_edge, right_edge, waves = pair_step(
                *received, window, packed, waves, turn, 0
            )
            pairs = range(PAIR_ROWS)
            low, high = hop(right_edge, pairs, 0, 1), hop(left_edge, pairs, 0, -1)
            out, waves = pair_step(low, left_edge, high, window, packed, waves, turn, 2)
            if turn + 1 == PAIR_ROWS:
                down_rows = (PAIR_ROWS, chip_rows)
                packed = pack_halo(
                    gated(ids, out), halo, packed, down_rows, DOWN_SLOTS, "halo_down", False
                )
                _, early_halo = send_halo(gated(ids, out, *halo), other, early_parts, "cut_early")
                out, packed = lax.optimization_barrier((out, packed))
        else:
            out, waves = down_step(received, window, packed, waves, turn)
            if turn == LATE_ROWS:
                late_ids, last_rows = gated(ids, out), (LATE_ROWS + 1, chip_rows)
                packed = pack_halo(late_ids, early_halo, packed, last_rows, EARLY_SLOTS, "halo_last")
                out, packed = lax.optimization_barrier((out, packed))
                _, late_halo = send_halo(gated(ids, out), other, late_parts, "cut_late")
        if turn + 1 < chip_rows:
            group = range(turn % 3, chip_rows, 3)
            received = (hop(out, group, 1, 1), hop(out, group, 1, 0), hop(out, group, 1, -1))

    deep = waves[2:, :, HALO * TILE : (HALO + OWN) * TILE]
    left, right = hop(deep, everyone, 0, 1), hop(deep, everyone, 0, -1)
    received = (zero_half,) * 3
    for turn in reversed(everyone):
        out, field = up_step(received, window, packed, waves, left, right, field, turn)
        if turn == LATE_ROWS + 1:
            row = (LATE_ROWS, LATE_ROWS + 1)
            packed = pack_halo(gated(ids, out), early_halo, packed, row, EARLY_SLOTS, "halo_early")
            out, packed = lax.optimization_barrier((out, packed))
        if turn == LATE_ROWS:
            late_rows = (0, LATE_ROWS)
            packed = pack_halo(gated(ids, out), late_halo, packed, late_rows, EARLY_SLOTS, "halo_late")
            out, packed = lax.optimization_barrier((out, packed))
        if turn == LATE_ROWS - 1:
            _, last_halo = send_halo(gated(ids, out), factor, last_parts, "cut_last", (0,))
        if turn == PAIR_ROWS:
            last_rows = (0, PAIR_ROWS)
            packed = pack_halo(
                gated(ids, out), last_halo, packed, last_rows, LAST_SLOTS, "halo_extra", False
            )
            out, packed = lax.optimization_barrier((out, packed))
        if turn:
            group = range(turn % 3, chip_rows, 3)
            received = (hop(out, group, -1, 1), hop(out, group, -1, 0), hop(out, group, -1, -1))

    shape = (2, layer_total, 2 * shot_count, HALF)
    waves = gated(waves, field)
    give = small_call(give_body, (ids,), (waves, field), shape, "give")
    taken = lax.ppermute(give, AXES, partner)
    return join(ids, waves, field, taken, rhs_field.shape)


def solution(mesh):
    placed = (
        P(None, "depth", None, "lat"),
        P(),
        P(),
        P("depth", "lat", None, None, None, None),
        P(None, None, "depth", "lat"),
    )
    return jax.shard_map(
        shards,
        mesh=mesh,
        in_specs=placed,
        out_specs=(P(None, "depth", None, "lat"), P(None, "depth", None, "lat")),
        check_vma=False,
    )
```

```python
import functools

import jax
import jax.numpy as jnp
from jax import lax
from jax.experimental import pallas as pl
from jax.experimental.pallas import tpu as pltpu
from jax.sharding import PartitionSpec as P

TILE = 128
GROUP = 4
OWN = 4
HALO = 3
SLOTS = OWN + 2 * HALO
WINDOW = (OWN + 2 * (HALO + 1)) * TILE
SPAN = SLOTS * TILE
HALF = OWN * TILE
VMEM_LIMIT = 10 << 20

VMEM_SPEC = pl.BlockSpec(memory_space=pltpu.VMEM)
SMEM_SPEC = pl.BlockSpec(memory_space=pltpu.SMEM)
ANY_SPEC = pl.BlockSpec(memory_space=pl.ANY)
PARAMS = pltpu.CompilerParams(vmem_limit_bytes=VMEM_LIMIT)
BRIEF = pl.CostEstimate(flops=1, transcendentals=0, bytes_accessed=1)
AXES = ("depth", "lat")


def chip_row():
    return lax.axis_index("depth") // 2


def chip_core():
    return lax.rem(lax.axis_index("depth"), 2)


def split_store(buffer, slot_ref):
    for offset in range(3):
        for part in range(2):
            block = buffer[offset, part]
            high = block.astype(jnp.bfloat16)
            low = (block - high.astype(jnp.float32)).astype(jnp.bfloat16)
            rows = slice(offset * TILE, (offset + 1) * TILE)
            slot_ref[rows, part * TILE : (part + 1) * TILE] = high
            slot_ref[rows, (2 + part) * TILE : (3 + part) * TILE] = low


BUFFERS = 4


def pipelined(units, start, sample, slot_of, buffers, sems):
    for ahead in range(BUFFERS - 1):

        @pl.when(ahead < units)
        def _():
            start(ahead, buffers.at[ahead], sems.at[ahead])

    def body(unit, _):
        place = lax.rem(unit, BUFFERS)
        later = lax.rem(unit + BUFFERS - 1, BUFFERS)

        @pl.when(unit + BUFFERS - 1 < units)
        def _():
            start(unit + BUFFERS - 1, buffers.at[later], sems.at[later])

        pltpu.make_async_copy(sample, buffers.at[place], sems.at[place]).wait()
        split_store(buffers.at[place], slot_of(unit))
        return 0

    lax.fori_loop(0, units, body, 0)


def chip_body(ids, source, *refs, mine):
    packed, buffers, sems = refs[-3:]
    core = chip_core()
    first = 2 * core if mine else 2 * (1 - core)
    count = OWN + HALO

    def start(unit, buffer, sem):
        block = source.at[unit // count, lax.rem(unit, count) + core]
        pltpu.make_async_copy(block, buffer, sem).start()

    def slot_of(unit):
        return packed.at[first + unit // count, lax.rem(unit, count) + HALO * (1 - core)]

    pipelined(2 * count, start, source.at[0, 0], slot_of, buffers, sems)


def pick(number, values):
    result = jnp.int32(values[0])
    for index, value in enumerate(values[1:], 1):
        result = jnp.where(number == index, value, result)
    return result


def halo_body(ids, straight, cross, *refs, rows, slots, split):
    packed, buffers, sems = refs[-3:]
    row, core = chip_row(), chip_core()
    units = len(slots[0])
    first = units // 2

    def start(unit, buffer, sem):
        by_straight = unit < first if split else core == 0
        place = lax.rem(unit, first) if split else unit

        @pl.when(by_straight)
        def _():
            pltpu.make_async_copy(straight.at[place], buffer, sem).start()

        @pl.when(jnp.logical_not(by_straight))
        def _():
            pltpu.make_async_copy(cross.at[place], buffer, sem).start()

    def slot_of(unit):
        number = unit + units * core
        return packed.at[
            pick(number, [layer for side in slots for layer, _ in side]),
            pick(number, [slot for side in slots for _, slot in side]),
        ]

    @pl.when((row >= rows[0]) & (row < rows[1]))
    def _():
        pipelined(units, start, straight.at[0], slot_of, buffers, sems)


PACKED = (GROUP, SLOTS, 3 * TILE, 4 * TILE)
PACK_SCRATCH = [
    pltpu.VMEM((BUFFERS, 3, 2, TILE, TILE), jnp.float32),
    pltpu.SemaphoreType.DMA((BUFFERS,)),
]


def pack_chip(ids, source, packed, mine):
    extra = () if packed is None else (packed,)
    return pl.pallas_call(
        functools.partial(chip_body, mine=mine),
        in_specs=[ANY_SPEC, ANY_SPEC] + [VMEM_SPEC] * len(extra),
        out_specs=VMEM_SPEC,
        out_shape=jax.ShapeDtypeStruct(PACKED, jnp.bfloat16),
        scratch_shapes=PACK_SCRATCH,
        input_output_aliases={2: 0} if extra else {},
        compiler_params=PARAMS,
        cost_estimate=BRIEF,
        name="pack_mine" if mine else "pack_partner",
    )(ids, pltpu.with_memory_space_constraint(source, pltpu.HBM) if mine else source, *extra)


def pack_halo(ids, sources, packed, rows, slots, name, split=True):
    return pl.pallas_call(
        functools.partial(halo_body, rows=rows, slots=slots, split=split),
        in_specs=[ANY_SPEC, ANY_SPEC, ANY_SPEC, VMEM_SPEC],
        out_specs=VMEM_SPEC,
        out_shape=jax.ShapeDtypeStruct(PACKED, jnp.bfloat16),
        scratch_shapes=PACK_SCRATCH,
        input_output_aliases={3: 0},
        compiler_params=PARAMS,
        cost_estimate=BRIEF,
        name=name,
    )(ids, *sources, packed)


def cut_body(ids, mine, other, straight, cross, sems, *, parts):
    row = chip_row()
    for begin_row, end_row, runs in parts:
        for side in range(2):

            @pl.when((row >= begin_row) & (row < end_row) & (chip_core() == side))
            def _():
                copies = []
                for out, entries in zip((straight, cross), runs[side]):
                    place = 0
                    for layer, begin, end in entries:
                        source = mine if layer // 2 == side else other
                        target = out.at[place : place + end - begin]
                        copies.append(
                            pltpu.make_async_copy(
                                source.at[layer % 2, begin:end], target, sems.at[len(copies)]
                            )
                        )
                        place += end - begin
                for copy in copies:
                    copy.start()
                for copy in copies:
                    copy.wait()


def cut(ids, mine, other, parts, name):
    count = sum(end - begin for _, begin, end in parts[0][2][0][0])
    return pl.pallas_call(
        functools.partial(cut_body, parts=parts),
        in_specs=[ANY_SPEC, ANY_SPEC, ANY_SPEC],
        out_specs=[ANY_SPEC] * 2,
        out_shape=[pltpu.VMEM((count, 3, 2, TILE, TILE), jnp.float32)] * 2,
        scratch_shapes=[pltpu.SemaphoreType.DMA((6,))],
        compiler_params=PARAMS,
        cost_estimate=BRIEF,
        name=name,
    )(ids, pltpu.with_memory_space_constraint(mine, pltpu.HBM), other)


ROWS = 20


def rows_body(ids, cells, layers, rhs, couple, rows):
    strip = rhs.shape[-1]
    shot = lax.broadcasted_iota(jnp.int32, (8, strip), 0)
    position = lax.broadcasted_iota(jnp.int32, (8, strip), 1) + lax.axis_index("lat") * strip
    target = jnp.full((8, strip), -1, jnp.int32)
    depth = jnp.full((8, strip), -1, jnp.int32)
    for index in range(8):
        target = jnp.where(shot == index, cells[index], target)
        depth = jnp.where(shot == index, layers[index], depth)
    here = target == position
    for layer in range(2):
        hit = here & (depth == lax.axis_index("depth") * 2 + layer)
        rows[layer, 0:8] = rhs[0, layer] + jnp.where(hit, 4.0, 0.0)
        rows[layer, 8:16] = rhs[1, layer]
        for way in range(2):
            for part in range(2):
                spot = 16 + 2 * way + part
                rows[layer, spot : spot + 1] = couple[way, part, layer : layer + 1]


def edge_body(ids, rows, other, edge):
    for side in range(2):

        @pl.when(chip_core() == side)
        def _():
            mine, partner = slice(2 * side, 2 * side + 2), slice(2 - 2 * side, 4 - 2 * side)
            where = slice(HALF, 2 * HALF) if side == 0 else slice(0, HALF)
            edge[mine] = rows[:, :, where]
            edge[partner] = other[:, :, where]


def window_body(ids, rows, other, beside, window):
    for side in range(2):

        @pl.when(chip_core() == side)
        def _():
            mine, partner = slice(2 * side, 2 * side + 2), slice(2 - 2 * side, 4 - 2 * side)
            chip = slice(HALF, WINDOW) if side == 0 else slice(0, 2 * HALF)
            rest = slice(0, HALF) if side == 0 else slice(2 * HALF, WINDOW)
            window[mine, :, chip] = rows[...]
            window[partner, :, chip] = other[...]
            window[:, :, rest] = beside[...]


def small_call(body, smem, arrays, shape, name):
    return pl.pallas_call(
        body,
        in_specs=[ANY_SPEC] + [SMEM_SPEC] * (len(smem) - 1) + [VMEM_SPEC] * len(arrays),
        out_specs=VMEM_SPEC,
        out_shape=jax.ShapeDtypeStruct(shape, jnp.float32),
        compiler_params=PARAMS,
        cost_estimate=BRIEF,
        name=name,
    )(*smem, *arrays)


def store_parts(parts_ref, where, value):
    high = value.astype(jnp.bfloat16)
    parts_ref[0:16, where] = high
    parts_ref[16:32, where] = (value - high.astype(jnp.float32)).astype(jnp.bfloat16)


def scaled(coef_real, coef_imag, value):
    real, imag = value[0:8], value[8:16]
    return jnp.concatenate(
        [coef_real * real - coef_imag * imag, coef_real * imag + coef_imag * real], axis=0
    )


def tile_product(parts_ref, packed, layer, spot):
    product = jnp.dot(
        parts_ref[:, spot * TILE : (spot + 3) * TILE],
        packed[layer, spot],
        preferred_element_type=jnp.float32,
    )
    rows = product[0:16] + product[16:32]
    both = rows[:, 0 : 2 * TILE] + rows[:, 2 * TILE : 4 * TILE]
    real, imag = both[0:8], both[8:16]
    return jnp.concatenate(
        [real[:, 0:TILE] - imag[:, TILE:], real[:, TILE:] + imag[:, 0:TILE]], axis=0
    )


def lanes(start, stop):
    return slice(start * TILE, stop * TILE)


def down_operand(parts, window, layer, where, value):
    forcing = window[layer, 0:16, where]
    coef_real, coef_imag = window[layer, 16:17, where], window[layer, 17:18, where]
    store_parts(parts.at[layer % 2], where, forcing + scaled(coef_real, coef_imag, value))


def up_operand(parts, window, layer, where, value):
    coef_real, coef_imag = window[layer, 18:19, where], window[layer, 19:20, where]
    store_parts(parts.at[layer % 2], where, scaled(coef_real, coef_imag, value))


def down_layers(window, packed, waves, parts, layers):
    for layer in layers:
        reach = layers[-1] - layer
        for spot in range(HALO - reach, HALO + OWN + reach):
            value = tile_product(parts.at[layer % 2], packed, layer, spot)
            waves[layer, :, lanes(spot, spot + 1)] = value
            if reach:
                down_operand(parts, window, layer + 1, lanes(spot + 1, spot + 2), value)


def my_turn(turn):
    return chip_row() == turn


def down_body(low, mid, high, window, packed, _, out, waves, parts, *, turn):
    @pl.when(my_turn(turn))
    def _():
        for index, source in enumerate((low, mid, high)):
            down_operand(parts, window, 0, lanes(4 * index, 4 * index + 4), source[...])
        down_layers(window, packed, waves, parts, range(GROUP))
        out[...] = waves[GROUP - 1, :, lanes(HALO, HALO + OWN)]


def pair_body(low, mid, high, window, packed, _, *refs, turn, first):
    outs, waves, parts = refs[:-2], refs[-2], refs[-1]

    @pl.when(my_turn(turn))
    def _():
        if first:
            waves[1, :, lanes(1, 3)] = low[...]
            waves[1, :, lanes(7, 9)] = high[...]
            down_operand(parts, window, first, lanes(2, 10), waves[1, :, lanes(1, 9)])
        else:
            down_operand(parts, window, first, lanes(2, 4), low[:, lanes(2, 4)])
            down_operand(parts, window, first, lanes(4, 8), mid[...])
            down_operand(parts, window, first, lanes(8, 10), high[:, lanes(0, 2)])
        down_layers(window, packed, waves, parts, (first, first + 1))
        if first:
            outs[0][...] = waves[3, :, lanes(HALO, HALO + OWN)]
        else:
            outs[0][...] = waves[1, :, lanes(HALO, HALO + 2)]
            outs[1][...] = waves[1, :, lanes(HALO + 2, HALO + OWN)]


def up_body(low, mid, high, window, packed, waves, left, right, _, out, field, parts, *, turn):
    @pl.when(my_turn(turn))
    def _():
        for index, source in enumerate((low, mid, high)):
            up_operand(parts, window, GROUP - 1, lanes(4 * index, 4 * index + 4), source[...])
        for layer in reversed(range(GROUP)):
            for spot in range(HALO - layer, HALO + OWN + layer):
                if layer >= 2 and spot < HALO:
                    wave = left[layer - 2, :, lanes(spot + 1, spot + 2)]
                elif layer >= 2 and spot >= HALO + OWN:
                    wave = right[layer - 2, :, lanes(spot - HALO - OWN, spot - HALO - OWN + 1)]
                else:
                    wave = waves[layer, :, lanes(spot, spot + 1)]
                value = wave + tile_product(parts.at[layer % 2], packed, layer, spot)
                if layer:
                    up_operand(parts, window, layer - 1, lanes(spot + 1, spot + 2), value)
                if HALO <= spot < HALO + OWN:
                    field[layer, :, lanes(spot - HALO, spot - HALO + 1)] = value
        out[...] = field[0]


PARTS = pltpu.VMEM((2, 32, WINDOW), jnp.bfloat16)


def down_step(received, window, packed, waves, turn):
    return pl.pallas_call(
        functools.partial(down_body, turn=turn),
        in_specs=[VMEM_SPEC] * 6,
        out_specs=(VMEM_SPEC, VMEM_SPEC),
        out_shape=(
            jax.ShapeDtypeStruct((16, HALF), jnp.float32),
            jax.ShapeDtypeStruct((GROUP, 16, SPAN), jnp.float32),
        ),
        scratch_shapes=[PARTS],
        input_output_aliases={5: 1},
        compiler_params=PARAMS,
        cost_estimate=BRIEF,
        name=f"down_{turn}",
    )(*received, window, packed, waves)


def pair_step(low, mid, high, window, packed, waves, turn, first):
    widths = (HALF,) if first else (2 * TILE, 2 * TILE)
    return pl.pallas_call(
        functools.partial(pair_body, turn=turn, first=first),
        in_specs=[VMEM_SPEC] * 6,
        out_specs=(VMEM_SPEC,) * (len(widths) + 1),
        out_shape=tuple(jax.ShapeDtypeStruct((16, width), jnp.float32) for width in widths)
        + (jax.ShapeDtypeStruct((GROUP, 16, SPAN), jnp.float32),),
        scratch_shapes=[PARTS],
        input_output_aliases={5: len(widths)},
        compiler_params=PARAMS,
        cost_estimate=BRIEF,
        name=f"pair_{turn}_{first}",
    )(low, mid, high, window, packed, waves)


def up_step(received, window, packed, waves, left, right, field, turn):
    return pl.pallas_call(
        functools.partial(up_body, turn=turn),
        in_specs=[VMEM_SPEC] * 9,
        out_specs=(VMEM_SPEC, VMEM_SPEC),
        out_shape=(
            jax.ShapeDtypeStruct((16, HALF), jnp.float32),
            jax.ShapeDtypeStruct((GROUP, 16, HALF), jnp.float32),
        ),
        scratch_shapes=[PARTS],
        input_output_aliases={8: 1},
        compiler_params=PARAMS,
        cost_estimate=BRIEF,
        name=f"up_{turn}",
    )(*received, window, packed, waves, left, right, field)


def give_body(ids, waves, field, give):
    own = slice(HALO * TILE, (HALO + OWN) * TILE)
    for side in range(2):

        @pl.when(chip_core() == side)
        def _():
            partner = slice(2 - 2 * side, 4 - 2 * side)
            give[0] = waves[partner, :, own]
            give[1] = field[partner]


def join_body(ids, waves, field, taken, out_waves, out_field):
    for side in range(2):

        @pl.when(chip_core() == side)
        def _():
            mine = slice(HALF * side, HALF * (side + 1))
            partner = slice(HALF * (1 - side), HALF * (2 - side))
            for layer in range(2):
                for part in range(2):
                    rows = slice(8 * part, 8 * (part + 1))
                    own = slice(HALO * TILE, (HALO + OWN) * TILE)
                    out_waves[part, layer, :, mine] = waves[2 * side + layer, rows, own]
                    out_field[part, layer, :, mine] = field[2 * side + layer, rows]
                    out_waves[part, layer, :, partner] = taken[0, layer, rows]
                    out_field[part, layer, :, partner] = taken[1, layer, rows]


def join(ids, waves, field, taken, shape):
    return pl.pallas_call(
        join_body,
        in_specs=[ANY_SPEC] + [VMEM_SPEC] * 3,
        out_specs=(VMEM_SPEC,) * 2,
        out_shape=(jax.ShapeDtypeStruct(shape, jnp.float32),) * 2,
        compiler_params=PARAMS,
        cost_estimate=BRIEF,
        name="join",
    )(ids, waves, field, taken)


PAIR_ROWS = 2
LATE_ROWS = 5
FIRST_RUNS = (
    (((0, 7, 8),), ((0, 0, 1),)),
    (((2, 0, 1),), ((2, 7, 8),)),
)
FIRST_SLOTS = (((0, 2), (2, 2)), ((2, 7), (0, 7)))
DOWN_RUNS = (
    (((0, 5, 7), (1, 6, 8)), ((0, 1, 3), (1, 0, 2))),
    ((), ()),
)
DOWN_SLOTS = (
    ((0, 0), (0, 1), (1, 1), (1, 2)),
    ((0, 8), (0, 9), (1, 7), (1, 8)),
)
EARLY_RUNS = (
    (((3, 7, 8), (2, 6, 7)), ((3, 0, 1), (2, 1, 2))),
    (((3, 1, 3),), ((3, 5, 7),)),
)
EARLY_SLOTS = (
    ((3, 2), (2, 1), (3, 0), (3, 1)),
    ((3, 8), (3, 9), (3, 7), (2, 8)),
)
LAST_RUNS = ((((1, 7, 8),), ((1, 0, 1),)), ((), ()))
LAST_SLOTS = (((1, 2),), ((1, 7),))


def gated(value, *others):
    return lax.optimization_barrier((value, *others))[0]


def shards(rhs_field, src_cell, src_layer, factor, couple):
    layer_total, shot_count, strip_cells = rhs_field.shape[1:]
    depth_count, lat_count = lax.axis_size("depth"), lax.axis_size("lat")
    depth_pos, lat_pos = lax.axis_index("depth"), lax.axis_index("lat")
    core = lax.rem(depth_pos, 2)
    first_core = core == 0
    chip_rows = depth_count // 2
    halves = 2 * lat_count
    everyone = range(chip_rows)
    ids = jnp.stack([depth_pos // 2, core, lat_pos, depth_pos]).astype(jnp.int32)

    def device(row, half):
        return (2 * row + half % 2) * lat_count + half // 2

    def at(depth, lat):
        return depth * lat_count + lat

    def hop(value, rows, step, shift):
        pairs = [
            (device(row, half), device(row + step, half + shift))
            for row in rows
            if 0 <= row + step < chip_rows
            for half in range(halves)
            if 0 <= half + shift < halves
        ]
        return lax.ppermute(value, AXES, pairs)

    partner = [(at(d, l), at(d ^ 1, l)) for d in range(depth_count) for l in range(lat_count)]

    def beside_pairs(rows, same, sides=(0, 1)):
        pairs = []
        for row in rows:
            for side in sides:
                shift = 1 if (side == 0) == same else -1
                target = side if same else 1 - side
                pairs += [
                    (at(2 * row + side, l), at(2 * row + target, l + shift))
                    for l in range(lat_count)
                    if 0 <= l + shift < lat_count
                ]
        return pairs

    def send_halo(ids, other, parts, name, sides=(0, 1), after=()):
        straight, cross = cut(ids, factor, other, parts, name)
        straight, cross = lax.optimization_barrier((straight, cross, *after))[:2]
        rows = [row for begin, end, _ in parts for row in range(begin, end)]
        return straight, (
            lax.ppermute(straight, AXES, beside_pairs(rows, True, sides)),
            lax.ppermute(cross, AXES, beside_pairs(rows, False, sides)),
        )

    first_cut, first_halo = send_halo(ids, factor, ((0, chip_rows, FIRST_RUNS),), "cut_first")
    down_parts = ((PAIR_ROWS, chip_rows, DOWN_RUNS),)
    early_parts = ((LATE_ROWS, chip_rows, EARLY_RUNS),)
    late_parts = ((0, LATE_ROWS, EARLY_RUNS),)
    last_parts = ((0, PAIR_ROWS, LAST_RUNS),)
    other = lax.ppermute(gated(factor, first_cut), AXES, partner)

    rows = small_call(
        rows_body,
        (gated(ids, first_cut), src_cell, src_layer),
        (rhs_field, couple),
        (layer_total, ROWS, strip_cells),
        "rows",
    )
    rows_other = lax.ppermute(rows, AXES, partner)
    packed = pack_chip(gated(ids, rows), factor, None, True)
    edge = small_call(
        edge_body, (gated(ids, packed),), (rows, rows_other), (GROUP, ROWS, HALF), "edge"
    )
    packed = pack_chip(ids, other, packed, False)
    beside = lax.ppermute(edge, AXES, beside_pairs(everyone, True))
    window = small_call(
        window_body, (gated(ids, packed, *first_halo),), (rows, rows_other, beside), (GROUP, ROWS, WINDOW), "window"
    )
    _, halo = send_halo(gated(ids, rows), factor, down_parts, "cut_down", (0,), (window, *first_halo))
    packed = pack_halo(
        gated(ids, window), first_halo, packed, (0, chip_rows), FIRST_SLOTS, "halo_first"
    )

    zero_half = jnp.zeros((2 * shot_count, HALF), jnp.float32)
    waves = jnp.zeros((GROUP, 2 * shot_count, SPAN), jnp.float32)
    field = jnp.zeros((GROUP, 2 * shot_count, HALF), jnp.float32)

    received = (zero_half,) * 3
    for turn in everyone:
        if turn < PAIR_ROWS:
            left_edge, right_edge, waves = pair_step(
                *received, window, packed, waves, turn, 0
            )
            pairs = range(PAIR_ROWS)
            low, high = hop(right_edge, pairs, 0, 1), hop(left_edge, pairs, 0, -1)
            out, waves = pair_step(low, left_edge, high, window, packed, waves, turn, 2)
            if turn + 1 == PAIR_ROWS:
                down_rows = (PAIR_ROWS, chip_rows)
                packed = pack_halo(
                    gated(ids, out), halo, packed, down_rows, DOWN_SLOTS, "halo_down", False
                )
                _, early_halo = send_halo(gated(ids, out, *halo), other, early_parts, "cut_early")
                out, packed = lax.optimization_barrier((out, packed))
        else:
            out, waves = down_step(received, window, packed, waves, turn)
            if turn == LATE_ROWS:
                late_ids, last_rows = gated(ids, out), (LATE_ROWS + 1, chip_rows)
                packed = pack_halo(late_ids, early_halo, packed, last_rows, EARLY_SLOTS, "halo_last")
                out, packed = lax.optimization_barrier((out, packed))
                _, late_halo = send_halo(gated(ids, out), other, late_parts, "cut_late")
        if turn + 1 < chip_rows:
            group = range(turn % 3, chip_rows, 3)
            received = (hop(out, group, 1, 1), hop(out, group, 1, 0), hop(out, group, 1, -1))

    deep = waves[2:, :, HALO * TILE : (HALO + OWN) * TILE]
    left, right = hop(deep, everyone, 0, 1), hop(deep, everyone, 0, -1)
    received = (zero_half,) * 3
    for turn in reversed(everyone):
        out, field = up_step(received, window, packed, waves, left, right, field, turn)
        if turn == LATE_ROWS + 1:
            row = (LATE_ROWS, LATE_ROWS + 1)
            packed = pack_halo(gated(ids, out), early_halo, packed, row, EARLY_SLOTS, "halo_early")
            out, packed = lax.optimization_barrier((out, packed))
        if turn == LATE_ROWS:
            late_rows = (0, LATE_ROWS)
            packed = pack_halo(gated(ids, out), late_halo, packed, late_rows, EARLY_SLOTS, "halo_late")
            out, packed = lax.optimization_barrier((out, packed))
        if turn == LATE_ROWS - 1:
            _, last_halo = send_halo(gated(ids, out), factor, last_parts, "cut_last", (0,))
        if turn == PAIR_ROWS:
            last_rows = (0, PAIR_ROWS)
            packed = pack_halo(
                gated(ids, out), last_halo, packed, last_rows, LAST_SLOTS, "halo_extra", False
            )
            out, packed = lax.optimization_barrier((out, packed))
        if turn:
            group = range(turn % 3, chip_rows, 3)
            received = (hop(out, group, -1, 1), hop(out, group, -1, 0), hop(out, group, -1, -1))

    shape = (2, layer_total, 2 * shot_count, HALF)
    waves = gated(waves, field)
    give = small_call(give_body, (ids,), (waves, field), shape, "give")
    taken = lax.ppermute(give, AXES, partner)
    return join(ids, waves, field, taken, rhs_field.shape)


def solution(mesh):
    placed = (
        P(None, "depth", None, "lat"),
        P(),
        P(),
        P("depth", "lat", None, None, None, None),
        P(None, None, "depth", "lat"),
    )
    return jax.shard_map(
        shards,
        mesh=mesh,
        in_specs=placed,
        out_specs=(P(None, "depth", None, "lat"), P(None, "depth", None, "lat")),
        check_vma=False,
    )
```

```python
import functools

import jax
import jax.numpy as jnp
from jax import lax
from jax.experimental import pallas as pl
from jax.experimental.pallas import tpu as pltpu
from jax.sharding import PartitionSpec as P

TILE = 128
GROUP = 4
OWN = 4
HALO = 3
SLOTS = OWN + 2 * HALO
WINDOW = (OWN + 2 * (HALO + 1)) * TILE
SPAN = SLOTS * TILE
HALF = OWN * TILE
VMEM_LIMIT = 10 << 20

VMEM_SPEC = pl.BlockSpec(memory_space=pltpu.VMEM)
SMEM_SPEC = pl.BlockSpec(memory_space=pltpu.SMEM)
ANY_SPEC = pl.BlockSpec(memory_space=pl.ANY)
PARAMS = pltpu.CompilerParams(vmem_limit_bytes=VMEM_LIMIT)
BRIEF = pl.CostEstimate(flops=1, transcendentals=0, bytes_accessed=1)
AXES = ("depth", "lat")


def chip_row():
    return lax.axis_index("depth") // 2


def chip_core():
    return lax.rem(lax.axis_index("depth"), 2)


def split_store(buffer, slot_ref):
    for offset in range(3):
        for part in range(2):
            block = buffer[offset, part]
            high = block.astype(jnp.bfloat16)
            low = (block - high.astype(jnp.float32)).astype(jnp.bfloat16)
            rows = slice(offset * TILE, (offset + 1) * TILE)
            slot_ref[rows, part * TILE : (part + 1) * TILE] = high
            slot_ref[rows, (2 + part) * TILE : (3 + part) * TILE] = low


BUFFERS = 4


def pipelined(units, start, sample, slot_of, buffers, sems):
    for ahead in range(BUFFERS - 1):

        @pl.when(ahead < units)
        def _():
            start(ahead, buffers.at[ahead], sems.at[ahead])

    def body(unit, _):
        place = lax.rem(unit, BUFFERS)
        later = lax.rem(unit + BUFFERS - 1, BUFFERS)

        @pl.when(unit + BUFFERS - 1 < units)
        def _():
            start(unit + BUFFERS - 1, buffers.at[later], sems.at[later])

        pltpu.make_async_copy(sample, buffers.at[place], sems.at[place]).wait()
        split_store(buffers.at[place], slot_of(unit))
        return 0

    lax.fori_loop(0, units, body, 0)


def chip_body(ids, source, *refs, mine):
    packed, buffers, sems = refs[-3:]
    core = chip_core()
    first = 2 * core if mine else 2 * (1 - core)
    count = OWN + HALO

    def start(unit, buffer, sem):
        block = source.at[unit // count, lax.rem(unit, count) + core]
        pltpu.make_async_copy(block, buffer, sem).start()

    def slot_of(unit):
        return packed.at[first + unit // count, lax.rem(unit, count) + HALO * (1 - core)]

    pipelined(2 * count, start, source.at[0, 0], slot_of, buffers, sems)


def pick(number, values):
    result = jnp.int32(values[0])
    for index, value in enumerate(values[1:], 1):
        result = jnp.where(number == index, value, result)
    return result


def halo_body(ids, straight, cross, *refs, rows, slots, split):
    packed, buffers, sems = refs[-3:]
    row, core = chip_row(), chip_core()
    units = len(slots[0])
    first = units // 2

    def start(unit, buffer, sem):
        by_straight = unit < first if split else core == 0
        place = lax.rem(unit, first) if split else unit

        @pl.when(by_straight)
        def _():
            pltpu.make_async_copy(straight.at[place], buffer, sem).start()

        @pl.when(jnp.logical_not(by_straight))
        def _():
            pltpu.make_async_copy(cross.at[place], buffer, sem).start()

    def slot_of(unit):
        number = unit + units * core
        return packed.at[
            pick(number, [layer for side in slots for layer, _ in side]),
            pick(number, [slot for side in slots for _, slot in side]),
        ]

    @pl.when((row >= rows[0]) & (row < rows[1]))
    def _():
        pipelined(units, start, straight.at[0], slot_of, buffers, sems)


PACKED = (GROUP, SLOTS, 3 * TILE, 4 * TILE)
PACK_SCRATCH = [
    pltpu.VMEM((BUFFERS, 3, 2, TILE, TILE), jnp.float32),
    pltpu.SemaphoreType.DMA((BUFFERS,)),
]


def pack_chip(ids, source, packed, mine):
    extra = () if packed is None else (packed,)
    return pl.pallas_call(
        functools.partial(chip_body, mine=mine),
        in_specs=[ANY_SPEC, ANY_SPEC] + [VMEM_SPEC] * len(extra),
        out_specs=VMEM_SPEC,
        out_shape=jax.ShapeDtypeStruct(PACKED, jnp.bfloat16),
        scratch_shapes=PACK_SCRATCH,
        input_output_aliases={2: 0} if extra else {},
        compiler_params=PARAMS,
        cost_estimate=BRIEF,
        name="pack_mine" if mine else "pack_partner",
    )(ids, pltpu.with_memory_space_constraint(source, pltpu.HBM) if mine else source, *extra)


def pack_halo(ids, sources, packed, rows, slots, name, split=True):
    return pl.pallas_call(
        functools.partial(halo_body, rows=rows, slots=slots, split=split),
        in_specs=[ANY_SPEC, ANY_SPEC, ANY_SPEC, VMEM_SPEC],
        out_specs=VMEM_SPEC,
        out_shape=jax.ShapeDtypeStruct(PACKED, jnp.bfloat16),
        scratch_shapes=PACK_SCRATCH,
        input_output_aliases={3: 0},
        compiler_params=PARAMS,
        cost_estimate=BRIEF,
        name=name,
    )(ids, *sources, packed)


def cut_body(ids, mine, other, straight, cross, sems, *, parts):
    row = chip_row()
    for begin_row, end_row, runs in parts:
        for side in range(2):

            @pl.when((row >= begin_row) & (row < end_row) & (chip_core() == side))
            def _():
                copies = []
                for out, entries in zip((straight, cross), runs[side]):
                    place = 0
                    for layer, begin, end in entries:
                        source = mine if layer // 2 == side else other
                        target = out.at[place : place + end - begin]
                        copies.append(
                            pltpu.make_async_copy(
                                source.at[layer % 2, begin:end], target, sems.at[len(copies)]
                            )
                        )
                        place += end - begin
                for copy in copies:
                    copy.start()
                for copy in copies:
                    copy.wait()


def cut(ids, mine, other, parts, name):
    count = sum(end - begin for _, begin, end in parts[0][2][0][0])
    return pl.pallas_call(
        functools.partial(cut_body, parts=parts),
        in_specs=[ANY_SPEC, ANY_SPEC, ANY_SPEC],
        out_specs=[ANY_SPEC] * 2,
        out_shape=[pltpu.VMEM((count, 3, 2, TILE, TILE), jnp.float32)] * 2,
        scratch_shapes=[pltpu.SemaphoreType.DMA((6,))],
        compiler_params=PARAMS,
        cost_estimate=BRIEF,
        name=name,
    )(ids, pltpu.with_memory_space_constraint(mine, pltpu.HBM), other)


ROWS = 20


def rows_body(ids, cells, layers, rhs, couple, rows):
    strip = rhs.shape[-1]
    shot = lax.broadcasted_iota(jnp.int32, (8, strip), 0)
    position = lax.broadcasted_iota(jnp.int32, (8, strip), 1) + lax.axis_index("lat") * strip
    target = jnp.full((8, strip), -1, jnp.int32)
    depth = jnp.full((8, strip), -1, jnp.int32)
    for index in range(8):
        target = jnp.where(shot == index, cells[index], target)
        depth = jnp.where(shot == index, layers[index], depth)
    here = target == position
    for layer in range(2):
        hit = here & (depth == lax.axis_index("depth") * 2 + layer)
        rows[layer, 0:8] = rhs[0, layer] + jnp.where(hit, 4.0, 0.0)
        rows[layer, 8:16] = rhs[1, layer]
        for way in range(2):
            for part in range(2):
                spot = 16 + 2 * way + part
                rows[layer, spot : spot + 1] = couple[way, part, layer : layer + 1]


def edge_body(ids, rows, other, edge):
    for side in range(2):

        @pl.when(chip_core() == side)
        def _():
            mine, partner = slice(2 * side, 2 * side + 2), slice(2 - 2 * side, 4 - 2 * side)
            where = slice(HALF, 2 * HALF) if side == 0 else slice(0, HALF)
            edge[mine] = rows[:, :, where]
            edge[partner] = other[:, :, where]


def window_body(ids, rows, other, beside, window):
    for side in range(2):

        @pl.when(chip_core() == side)
        def _():
            mine, partner = slice(2 * side, 2 * side + 2), slice(2 - 2 * side, 4 - 2 * side)
            chip = slice(HALF, WINDOW) if side == 0 else slice(0, 2 * HALF)
            rest = slice(0, HALF) if side == 0 else slice(2 * HALF, WINDOW)
            window[mine, :, chip] = rows[...]
            window[partner, :, chip] = other[...]
            window[:, :, rest] = beside[...]


def small_call(body, smem, arrays, shape, name):
    return pl.pallas_call(
        body,
        in_specs=[ANY_SPEC] + [SMEM_SPEC] * (len(smem) - 1) + [VMEM_SPEC] * len(arrays),
        out_specs=VMEM_SPEC,
        out_shape=jax.ShapeDtypeStruct(shape, jnp.float32),
        compiler_params=PARAMS,
        cost_estimate=BRIEF,
        name=name,
    )(*smem, *arrays)


def store_parts(parts_ref, where, value):
    high = value.astype(jnp.bfloat16)
    parts_ref[0:16, where] = high
    parts_ref[16:32, where] = (value - high.astype(jnp.float32)).astype(jnp.bfloat16)


def scaled(coef_real, coef_imag, value):
    real, imag = value[0:8], value[8:16]
    return jnp.concatenate(
        [coef_real * real - coef_imag * imag, coef_real * imag + coef_imag * real], axis=0
    )


def tile_product(parts_ref, packed, layer, spot):
    product = jnp.dot(
        parts_ref[:, spot * TILE : (spot + 3) * TILE],
        packed[layer, spot],
        preferred_element_type=jnp.float32,
    )
    rows = product[0:16] + product[16:32]
    both = rows[:, 0 : 2 * TILE] + rows[:, 2 * TILE : 4 * TILE]
    real, imag = both[0:8], both[8:16]
    return jnp.concatenate(
        [real[:, 0:TILE] - imag[:, TILE:], real[:, TILE:] + imag[:, 0:TILE]], axis=0
    )


def lanes(start, stop):
    return slice(start * TILE, stop * TILE)


def down_operand(parts, window, layer, where, value):
    forcing = window[layer, 0:16, where]
    coef_real, coef_imag = window[layer, 16:17, where], window[layer, 17:18, where]
    store_parts(parts.at[layer % 2], where, forcing + scaled(coef_real, coef_imag, value))


def up_operand(parts, window, layer, where, value):
    coef_real, coef_imag = window[layer, 18:19, where], window[layer, 19:20, where]
    store_parts(parts.at[layer % 2], where, scaled(coef_real, coef_imag, value))


def down_layers(window, packed, waves, parts, layers):
    for layer in layers:
        reach = layers[-1] - layer
        for spot in range(HALO - reach, HALO + OWN + reach):
            value = tile_product(parts.at[layer % 2], packed, layer, spot)
            waves[layer, :, lanes(spot, spot + 1)] = value
            if reach:
                down_operand(parts, window, layer + 1, lanes(spot + 1, spot + 2), value)


def my_turn(turn):
    return chip_row() == turn


def down_body(low, mid, high, window, packed, _, out, waves, parts, *, turn):
    @pl.when(my_turn(turn))
    def _():
        for index, source in enumerate((low, mid, high)):
            down_operand(parts, window, 0, lanes(4 * index, 4 * index + 4), source[...])
        down_layers(window, packed, waves, parts, range(GROUP))
        out[...] = waves[GROUP - 1, :, lanes(HALO, HALO + OWN)]


def pair_body(low, mid, high, window, packed, _, *refs, turn, first):
    outs, waves, parts = refs[:-2], refs[-2], refs[-1]

    @pl.when(my_turn(turn))
    def _():
        if first:
            waves[1, :, lanes(1, 3)] = low[...]
            waves[1, :, lanes(7, 9)] = high[...]
            down_operand(parts, window, first, lanes(2, 10), waves[1, :, lanes(1, 9)])
        else:
            down_operand(parts, window, first, lanes(2, 4), low[:, lanes(2, 4)])
            down_operand(parts, window, first, lanes(4, 8), mid[...])
            down_operand(parts, window, first, lanes(8, 10), high[:, lanes(0, 2)])
        down_layers(window, packed, waves, parts, (first, first + 1))
        if first:
            outs[0][...] = waves[3, :, lanes(HALO, HALO + OWN)]
        else:
            outs[0][...] = waves[1, :, lanes(HALO, HALO + 2)]
            outs[1][...] = waves[1, :, lanes(HALO + 2, HALO + OWN)]


def up_body(low, mid, high, window, packed, waves, left, right, _, out, field, parts, *, turn):
    @pl.when(my_turn(turn))
    def _():
        for index, source in enumerate((low, mid, high)):
            up_operand(parts, window, GROUP - 1, lanes(4 * index, 4 * index + 4), source[...])
        for layer in reversed(range(GROUP)):
            for spot in range(HALO - layer, HALO + OWN + layer):
                if layer >= 2 and spot < HALO:
                    wave = left[layer - 2, :, lanes(spot + 1, spot + 2)]
                elif layer >= 2 and spot >= HALO + OWN:
                    wave = right[layer - 2, :, lanes(spot - HALO - OWN, spot - HALO - OWN + 1)]
                else:
                    wave = waves[layer, :, lanes(spot, spot + 1)]
                value = wave + tile_product(parts.at[layer % 2], packed, layer, spot)
                if layer:
                    up_operand(parts, window, layer - 1, lanes(spot + 1, spot + 2), value)
                if HALO <= spot < HALO + OWN:
                    field[layer, :, lanes(spot - HALO, spot - HALO + 1)] = value
        out[...] = field[0]


PARTS = pltpu.VMEM((2, 32, WINDOW), jnp.bfloat16)


def down_step(received, window, packed, waves, turn):
    return pl.pallas_call(
        functools.partial(down_body, turn=turn),
        in_specs=[VMEM_SPEC] * 6,
        out_specs=(VMEM_SPEC, VMEM_SPEC),
        out_shape=(
            jax.ShapeDtypeStruct((16, HALF), jnp.float32),
            jax.ShapeDtypeStruct((GROUP, 16, SPAN), jnp.float32),
        ),
        scratch_shapes=[PARTS],
        input_output_aliases={5: 1},
        compiler_params=PARAMS,
        cost_estimate=BRIEF,
        name=f"down_{turn}",
    )(*received, window, packed, waves)


def pair_step(low, mid, high, window, packed, waves, turn, first):
    widths = (HALF,) if first else (2 * TILE, 2 * TILE)
    return pl.pallas_call(
        functools.partial(pair_body, turn=turn, first=first),
        in_specs=[VMEM_SPEC] * 6,
        out_specs=(VMEM_SPEC,) * (len(widths) + 1),
        out_shape=tuple(jax.ShapeDtypeStruct((16, width), jnp.float32) for width in widths)
        + (jax.ShapeDtypeStruct((GROUP, 16, SPAN), jnp.float32),),
        scratch_shapes=[PARTS],
        input_output_aliases={5: len(widths)},
        compiler_params=PARAMS,
        cost_estimate=BRIEF,
        name=f"pair_{turn}_{first}",
    )(low, mid, high, window, packed, waves)


def up_step(received, window, packed, waves, left, right, field, turn):
    return pl.pallas_call(
        functools.partial(up_body, turn=turn),
        in_specs=[VMEM_SPEC] * 9,
        out_specs=(VMEM_SPEC, VMEM_SPEC),
        out_shape=(
            jax.ShapeDtypeStruct((16, HALF), jnp.float32),
            jax.ShapeDtypeStruct((GROUP, 16, HALF), jnp.float32),
        ),
        scratch_shapes=[PARTS],
        input_output_aliases={8: 1},
        compiler_params=PARAMS,
        cost_estimate=BRIEF,
        name=f"up_{turn}",
    )(*received, window, packed, waves, left, right, field)


def give_body(ids, waves, field, give):
    own = slice(HALO * TILE, (HALO + OWN) * TILE)
    for side in range(2):

        @pl.when(chip_core() == side)
        def _():
            partner = slice(2 - 2 * side, 4 - 2 * side)
            give[0] = waves[partner, :, own]
            give[1] = field[partner]


def join_body(ids, waves, field, taken, out_waves, out_field):
    for side in range(2):

        @pl.when(chip_core() == side)
        def _():
            mine = slice(HALF * side, HALF * (side + 1))
            partner = slice(HALF * (1 - side), HALF * (2 - side))
            for layer in range(2):
                for part in range(2):
                    rows = slice(8 * part, 8 * (part + 1))
                    own = slice(HALO * TILE, (HALO + OWN) * TILE)
                    out_waves[part, layer, :, mine] = waves[2 * side + layer, rows, own]
                    out_field[part, layer, :, mine] = field[2 * side + layer, rows]
                    out_waves[part, layer, :, partner] = taken[0, layer, rows]
                    out_field[part, layer, :, partner] = taken[1, layer, rows]


def join(ids, waves, field, taken, shape):
    return pl.pallas_call(
        join_body,
        in_specs=[ANY_SPEC] + [VMEM_SPEC] * 3,
        out_specs=(VMEM_SPEC,) * 2,
        out_shape=(jax.ShapeDtypeStruct(shape, jnp.float32),) * 2,
        compiler_params=PARAMS,
        cost_estimate=BRIEF,
        name="join",
    )(ids, waves, field, taken)


PAIR_ROWS = 3
LATE_ROWS = 5
FIRST_RUNS = (
    (((0, 7, 8),), ((0, 0, 1),)),
    (((2, 0, 1),), ((2, 7, 8),)),
)
FIRST_SLOTS = (((0, 2), (2, 2)), ((2, 7), (0, 7)))
DOWN_RUNS = (
    (((0, 5, 7), (1, 6, 8)), ((0, 1, 3), (1, 0, 2))),
    ((), ()),
)
DOWN_SLOTS = (
    ((0, 0), (0, 1), (1, 1), (1, 2)),
    ((0, 8), (0, 9), (1, 7), (1, 8)),
)
EARLY_RUNS = (
    (((3, 7, 8), (2, 6, 7)), ((3, 0, 1), (2, 1, 2))),
    (((3, 1, 3),), ((3, 5, 7),)),
)
EARLY_SLOTS = (
    ((3, 2), (2, 1), (3, 0), (3, 1)),
    ((3, 8), (3, 9), (3, 7), (2, 8)),
)
LAST_RUNS = ((((1, 7, 8),), ((1, 0, 1),)), ((), ()))
LAST_SLOTS = (((1, 2),), ((1, 7),))


def gated(value, *others):
    return lax.optimization_barrier((value, *others))[0]


def shards(rhs_field, src_cell, src_layer, factor, couple):
    layer_total, shot_count, strip_cells = rhs_field.shape[1:]
    depth_count, lat_count = lax.axis_size("depth"), lax.axis_size("lat")
    depth_pos, lat_pos = lax.axis_index("depth"), lax.axis_index("lat")
    core = lax.rem(depth_pos, 2)
    first_core = core == 0
    chip_rows = depth_count // 2
    halves = 2 * lat_count
    everyone = range(chip_rows)
    ids = jnp.stack([depth_pos // 2, core, lat_pos, depth_pos]).astype(jnp.int32)

    def device(row, half):
        return (2 * row + half % 2) * lat_count + half // 2

    def at(depth, lat):
        return depth * lat_count + lat

    def hop(value, rows, step, shift):
        pairs = [
            (device(row, half), device(row + step, half + shift))
            for row in rows
            if 0 <= row + step < chip_rows
            for half in range(halves)
            if 0 <= half + shift < halves
        ]
        return lax.ppermute(value, AXES, pairs)

    partner = [(at(d, l), at(d ^ 1, l)) for d in range(depth_count) for l in range(lat_count)]

    def beside_pairs(rows, same, sides=(0, 1)):
        pairs = []
        for row in rows:
            for side in sides:
                shift = 1 if (side == 0) == same else -1
                target = side if same else 1 - side
                pairs += [
                    (at(2 * row + side, l), at(2 * row + target, l + shift))
                    for l in range(lat_count)
                    if 0 <= l + shift < lat_count
                ]
        return pairs

    def send_halo(ids, other, parts, name, sides=(0, 1), after=()):
        straight, cross = cut(ids, factor, other, parts, name)
        straight, cross = lax.optimization_barrier((straight, cross, *after))[:2]
        rows = [row for begin, end, _ in parts for row in range(begin, end)]
        return straight, (
            lax.ppermute(straight, AXES, beside_pairs(rows, True, sides)),
            lax.ppermute(cross, AXES, beside_pairs(rows, False, sides)),
        )

    first_cut, first_halo = send_halo(ids, factor, ((0, chip_rows, FIRST_RUNS),), "cut_first")
    down_parts = ((PAIR_ROWS, chip_rows, DOWN_RUNS),)
    early_parts = ((LATE_ROWS, chip_rows, EARLY_RUNS),)
    late_parts = ((0, LATE_ROWS, EARLY_RUNS),)
    last_parts = ((0, PAIR_ROWS, LAST_RUNS),)
    other = lax.ppermute(gated(factor, first_cut), AXES, partner)

    rows = small_call(
        rows_body,
        (gated(ids, first_cut), src_cell, src_layer),
        (rhs_field, couple),
        (layer_total, ROWS, strip_cells),
        "rows",
    )
    rows_other = lax.ppermute(rows, AXES, partner)
    packed = pack_chip(gated(ids, rows), factor, None, True)
    edge = small_call(
        edge_body, (gated(ids, packed),), (rows, rows_other), (GROUP, ROWS, HALF), "edge"
    )
    packed = pack_chip(ids, other, packed, False)
    beside = lax.ppermute(edge, AXES, beside_pairs(everyone, True))
    window = small_call(
        window_body, (gated(ids, packed, *first_halo),), (rows, rows_other, beside), (GROUP, ROWS, WINDOW), "window"
    )
    _, halo = send_halo(gated(ids, rows), factor, down_parts, "cut_down", (0,), (window, *first_halo))
    packed = pack_halo(
        gated(ids, window), first_halo, packed, (0, chip_rows), FIRST_SLOTS, "halo_first"
    )

    zero_half = jnp.zeros((2 * shot_count, HALF), jnp.float32)
    waves = jnp.zeros((GROUP, 2 * shot_count, SPAN), jnp.float32)
    field = jnp.zeros((GROUP, 2 * shot_count, HALF), jnp.float32)

    received = (zero_half,) * 3
    for turn in everyone:
        if turn < PAIR_ROWS:
            left_edge, right_edge, waves = pair_step(
                *received, window, packed, waves, turn, 0
            )
            pairs = range(PAIR_ROWS)
            low, high = hop(right_edge, pairs, 0, 1), hop(left_edge, pairs, 0, -1)
            out, waves = pair_step(low, left_edge, high, window, packed, waves, turn, 2)
            if turn + 1 == PAIR_ROWS:
                down_rows = (PAIR_ROWS, chip_rows)
                packed = pack_halo(
                    gated(ids, out), halo, packed, down_rows, DOWN_SLOTS, "halo_down", False
                )
                _, early_halo = send_halo(gated(ids, out, *halo), other, early_parts, "cut_early")
                out, packed = lax.optimization_barrier((out, packed))
        else:
            out, waves = down_step(received, window, packed, waves, turn)
            if turn == LATE_ROWS:
                late_ids, last_rows = gated(ids, out), (LATE_ROWS + 1, chip_rows)
                packed = pack_halo(late_ids, early_halo, packed, last_rows, EARLY_SLOTS, "halo_last")
                out, packed = lax.optimization_barrier((out, packed))
                _, late_halo = send_halo(gated(ids, out), other, late_parts, "cut_late")
        if turn + 1 < chip_rows:
            group = range(turn % 3, chip_rows, 3)
            received = (hop(out, group, 1, 1), hop(out, group, 1, 0), hop(out, group, 1, -1))

    deep = waves[2:, :, HALO * TILE : (HALO + OWN) * TILE]
    left, right = hop(deep, everyone, 0, 1), hop(deep, everyone, 0, -1)
    received = (zero_half,) * 3
    for turn in reversed(everyone):
        out, field = up_step(received, window, packed, waves, left, right, field, turn)
        if turn == LATE_ROWS + 1:
            row = (LATE_ROWS, LATE_ROWS + 1)
            packed = pack_halo(gated(ids, out), early_halo, packed, row, EARLY_SLOTS, "halo_early")
            out, packed = lax.optimization_barrier((out, packed))
        if turn == LATE_ROWS:
            late_rows = (0, LATE_ROWS)
            packed = pack_halo(gated(ids, out), late_halo, packed, late_rows, EARLY_SLOTS, "halo_late")
            out, packed = lax.optimization_barrier((out, packed))
            _, last_halo = send_halo(gated(ids, out), factor, last_parts, "cut_last", (0,))
        if turn == PAIR_ROWS:
            last_rows = (0, PAIR_ROWS)
            packed = pack_halo(
                gated(ids, out), last_halo, packed, last_rows, LAST_SLOTS, "halo_extra", False
            )
            out, packed = lax.optimization_barrier((out, packed))
        if turn:
            group = range(turn % 3, chip_rows, 3)
            received = (hop(out, group, -1, 1), hop(out, group, -1, 0), hop(out, group, -1, -1))

    shape = (2, layer_total, 2 * shot_count, HALF)
    waves = gated(waves, field)
    give = small_call(give_body, (ids,), (waves, field), shape, "give")
    taken = lax.ppermute(give, AXES, partner)
    return join(ids, waves, field, taken, rhs_field.shape)


def solution(mesh):
    placed = (
        P(None, "depth", None, "lat"),
        P(),
        P(),
        P("depth", "lat", None, None, None, None),
        P(None, None, "depth", "lat"),
    )
    return jax.shard_map(
        shards,
        mesh=mesh,
        in_specs=placed,
        out_specs=(P(None, "depth", None, "lat"), P(None, "depth", None, "lat")),
        check_vma=False,
    )
```
